32 devices in a mesh: shot: 4 (over y, x), sub: 8 (over z, core).
Axes of the slice: x: 2, y: 2, z: 4, core: 2. Of those that a mesh axis runs over, the one named last changes fastest.
Arguments:
- courant: float32 [192, 64, 128], P('sub'), may hold values from 0.2 to 0.55
- lam_prev: float32 [4, 192, 64, 128], P('shot', 'sub'), may hold values from -6 to 6
- lam_cur: float32 [4, 192, 64, 128], P('shot', 'sub'), may hold values from -6 to 6
- accel: bfloat16 [4, 4, 192, 64, 128], P('shot', None, 'sub'), may hold values from -6 to 6
- traces: float32 [4, 4, 256], P('shot'), may hold values from -18 to 18
- receivers: int32 [4, 256, 3], P('shot'), may hold values from 0 to 191, as said below
- sources: int32 [4, 3], P('shot'), may hold values from 0 to 191, as said below
- smooth_x: float32 [192, 192], replicated
- smooth_y: float32 [64, 64], replicated
- smooth_z: float32 [128, 128], replicated
Outputs:
- gradient: float32 [192, 64, 128], P('shot', 'sub')
- lam_prev_out: float32 [4, 192, 64, 128], P('shot', 'sub')
- lam_cur_out: float32 [4, 192, 64, 128], P('shot', 'sub')
The draws below stay inside these ranges and needn't reach their ends.
Inputs may be any that keep to these rules, and one draw needn't show every extreme that they name: Each receiver lies in the grid: first coordinate below 192, second below 64, third below 128; several receivers may share a cell. `sources`: each source lies in the grid: first coordinate below 192, second below 64, third below 128.
All inputs are finite; a program needn't handle non-finite values.
Results may differ from the reference program's by a relative error of at most 0.0003.
Values sent between devices are 32-bit elements; how exact they have to be, the bound alone decides.
A program may use at most 64 MiB of HBM per device.

```python
import math
import jax
import jax.numpy as jnp
from jax import lax

NY = 64
NZ = 128
STEPS = 4
NREC = 256
TAPER = 8
SHOTS = 4
NX = 192


def smoother(key, count):
    rows = jnp.arange(count)[:, None].astype(jnp.float32)
    cols = jnp.arange(count)[None, :].astype(jnp.float32)
    reach = count / 4.0
    rough = jax.random.uniform(key, (count, count), jnp.float32, 0.7, 1.3)
    core = jnp.exp(-jnp.abs(rows - cols) / reach) * rough
    return (core + jnp.eye(count, dtype=jnp.float32)) / (2.0 * reach + 1.0)


def draw_smooth_x(key, part):
    return smoother(jax.random.fold_in(key, 11), NX)


def draw_smooth_y(key, part):
    return smoother(jax.random.fold_in(key, 12), NY)


def draw_smooth_z(key, part):
    return smoother(jax.random.fold_in(key, 13), NZ)


def draw_receivers(key, part):
    first = jax.random.randint(jax.random.fold_in(key, 1), (SHOTS, NREC, 1), 0, NX)
    second = jax.random.randint(jax.random.fold_in(key, 2), (SHOTS, NREC, 1), 0, NY)
    third = jax.random.randint(jax.random.fold_in(key, 3), (SHOTS, NREC, 1), 0, NZ)
    placed = jnp.concatenate([first, second, third], axis=2).astype(jnp.int32)
    corner = jnp.array([NX - 1, NY - 1, NZ - 1], dtype=jnp.int32)
    anchor = jnp.zeros((3,), dtype=jnp.int32)
    placed = placed.at[0, 0].set(corner)
    placed = placed.at[0, 1].set(anchor)
    return placed


def draw_sources(key, part):
    first = jax.random.randint(jax.random.fold_in(key, 4), (SHOTS, 1), 0, NX)
    second = jax.random.randint(jax.random.fold_in(key, 5), (SHOTS, 1), 0, NY)
    third = jax.random.randint(jax.random.fold_in(key, 6), (SHOTS, 1), 0, NZ)
    placed = jnp.concatenate([first, second, third], axis=1).astype(jnp.int32)
    corner = jnp.array([NX - 1, NY - 1, NZ - 1], dtype=jnp.int32)
    anchor = jnp.zeros((3,), dtype=jnp.int32)
    placed = placed.at[0].set(corner)
    placed = placed.at[1].set(anchor)
    return placed


def block_levels(key, dims, shards, low, top_value):
    gain, own = 1.0, jax.random.fold_in(key, 6)
    for dim, blocks in shards:
        heights = jnp.exp(jax.random.uniform(jax.random.fold_in(own, dim), (blocks,), jnp.float32, low / len(shards), top_value / len(shards)))
        gain = gain * jnp.repeat(heights, dims[dim] // blocks).reshape([-1 if axis == dim else 1 for axis in range(len(dims))])
    return gain


def gaussian(key, shape, spread, limit, cuts=(), held_as=jnp.bfloat16):
    entries = spread * jax.random.normal(key, shape, jnp.float32)
    if cuts:
        entries = entries * block_levels(key, shape, cuts, -0.22, 0.18)
    return jnp.clip(entries, -limit, limit).astype(held_as)


def setup_inputs(seed: int = 0) -> dict:
    keys = jax.random.split(jax.random.key(seed), 11)
    courant = jnp.clip(jnp.exp(math.log(0.55) - 1.011601 * jax.random.uniform(keys[0], (NX, NY, NZ), jnp.float32) ** block_levels(keys[0], (NX, NY, NZ), ((0, 8),), -0.2, 0.2)), 0.2, 0.55)
    lam_prev = gaussian(keys[1], (SHOTS, NX, NY, NZ), 1.0, 6.0, ((0, 4), (1, 8)), jnp.float32)
    lam_cur = gaussian(keys[2], (SHOTS, NX, NY, NZ), 1.0, 6.0, ((0, 4), (1, 8)), jnp.float32)
    accel = gaussian(keys[3], (SHOTS, STEPS, NX, NY, NZ), 1.0, 6.0, ((0, 4), (2, 8)))
    traces = gaussian(keys[4], (SHOTS, STEPS, NREC), 3.0, 18.0, ((0, 4),), jnp.float32)
    receivers = draw_receivers(jax.random.fold_in(keys[10], 71), 0)
    sources = draw_sources(jax.random.fold_in(keys[10], 71), 0)
    smooth_x = draw_smooth_x(jax.random.fold_in(keys[10], 71), 0)
    smooth_y = draw_smooth_y(jax.random.fold_in(keys[10], 71), 0)
    smooth_z = draw_smooth_z(jax.random.fold_in(keys[10], 71), 0)
    return {"courant": courant, "lam_prev": lam_prev, "lam_cur": lam_cur, "accel": accel, "traces": traces, "receivers": receivers, "sources": sources, "smooth_x": smooth_x, "smooth_y": smooth_y, "smooth_z": smooth_z}


def laplace(field):
    padded = jnp.pad(field, 1)
    beside = padded[2:, 1:-1, 1:-1] + padded[:-2, 1:-1, 1:-1]
    beside = beside + padded[1:-1, 2:, 1:-1] + padded[1:-1, :-2, 1:-1]
    beside = beside + padded[1:-1, 1:-1, 2:] + padded[1:-1, 1:-1, :-2]
    return beside - 6.0 * field


def reference(courant, lam_prev, lam_cur, accel, traces, receivers, sources, smooth_x, smooth_y, smooth_z):
    coeff = courant * courant
    xpos = jnp.arange(NX).astype(jnp.float32)[:, None, None]
    ypos = jnp.arange(NY).astype(jnp.float32)[None, :, None]
    zpos = jnp.arange(NZ).astype(jnp.float32)[None, None, :]

    def one_group(items):
        prev, cur, group_accel, group_traces, group_rec, group_src = items
        image = jnp.zeros_like(cur)
        for step in range(STEPS):
            fresh = 2.0 * cur - prev + coeff * laplace(cur)
            fresh = fresh.at[group_rec[:, 0], group_rec[:, 1], group_rec[:, 2]].add(group_traces[step])
            image = image + fresh * group_accel[step].astype(jnp.float32)
            prev, cur = cur, fresh
        source = group_src.astype(jnp.float32)
        dist = (xpos - source[0]) ** 2 + (ypos - source[1]) ** 2 + (zpos - source[2]) ** 2
        taper = 1.0 - jnp.exp(-dist / float(TAPER * TAPER))
        return prev, cur, image * taper

    prev_all, cur_all, images = lax.map(one_group, (lam_prev, lam_cur, accel, traces, receivers, sources))
    raw = jnp.sum(images, axis=0)
    high = lax.Precision.HIGHEST
    smoothed = jnp.einsum("abc,kc->abk", raw, smooth_z, precision=high)
    smoothed = jnp.einsum("abk,jb->ajk", smoothed, smooth_y, precision=high)
    smoothed = jnp.einsum("ajk,ia->ijk", smoothed, smooth_x, precision=high)
    return smoothed, prev_all, cur_all
```

```python
import functools

import jax
import jax.numpy as jnp
from jax import lax
from jax.experimental import pallas as pl
from jax.experimental.pallas import tpu as pltpu
from jax.sharding import PartitionSpec as P

STEPS = 4
TAPER = 8


def with_halo(value, sides, width):
    for axis, dim in sides:
        count, length = (lax.axis_size(axis), value.shape[dim])
        up = [(i, (i + 1) % count) for i in range(count - 1)]
        down = [(j, i) for i, j in up]
        last = lax.slice_in_dim(value, length - width, length, axis=dim)
        initial = lax.slice_in_dim(value, 0, width, axis=dim)
        before = lax.ppermute(last, axis, up)
        after = lax.ppermute(initial, axis, down)
        value = jnp.concatenate([before, value, after], axis=dim)
    return value


def plane_sum(block):
    side = jnp.pad(block, ((0, 0), (1, 1), (1, 1)))
    total = side[:, 2:, 1:-1] + side[:, :-2, 1:-1]
    return total + side[:, 1:-1, 2:] + side[:, 1:-1, :-2]


def inject(group_rec, weights, start, length, width_y, width_z):
    row_hit = (group_rec[None, :, 0] - start == jnp.arange(length)[:, None]).astype(jnp.float32)
    col_hit = (group_rec[None, :, 1] == jnp.arange(width_y)[:, None]).astype(jnp.float32)
    depth_hit = (group_rec[None, :, 2] == jnp.arange(width_z)[:, None]).astype(jnp.float32)
    plane = row_hit[:, None, :] * col_hit[None, :, :]
    depth_weight = depth_hit * weights[None, :]
    return jnp.einsum("abr,cr->abc", plane, depth_weight, precision=lax.Precision.HIGHEST)


def shards(
    courant, lam_prev, lam_cur, accel, traces, receivers, sources, smooth_x, smooth_y, smooth_z
):
    rows = courant.shape[0]
    width_y = courant.shape[1]
    width_z = courant.shape[2]
    first = lax.axis_index("sub") * rows
    coeff = courant * courant
    prev = lam_prev[0]
    cur = lam_cur[0]
    group_rec = receivers[0]
    image = jnp.zeros_like(cur)
    for step in range(STEPS):
        padded = with_halo(cur, (("sub", 0),), 1)
        beside = padded[2:] + padded[:-2] + plane_sum(cur)
        fresh = 2.0 * cur - prev + coeff * (beside - 6.0 * cur)
        fresh = fresh + inject(group_rec, traces[0, step], first, rows, width_y, width_z)
        image = image + fresh * accel[0, step].astype(jnp.float32)
        prev, cur = (cur, fresh)
    source = sources[0].astype(jnp.float32)
    xpos = (first + jnp.arange(rows)).astype(jnp.float32)[:, None, None]
    ypos = jnp.arange(width_y).astype(jnp.float32)[None, :, None]
    zpos = jnp.arange(width_z).astype(jnp.float32)[None, None, :]
    dist = (xpos - source[0]) ** 2 + (ypos - source[1]) ** 2 + (zpos - source[2]) ** 2
    image = image * (1.0 - jnp.exp(-dist / float(TAPER * TAPER)))
    high = lax.Precision.HIGHEST
    total = lax.psum(image, "shot")
    total = jnp.einsum("abc,kc->abk", total, smooth_z, precision=high)
    total = jnp.einsum("abk,jb->ajk", total, smooth_y, precision=high)
    lines = lax.all_to_all(total, "sub", split_axis=1, concat_axis=0, tiled=True)
    lines = jnp.einsum("ajk,ia->ijk", lines, smooth_x, precision=high)
    share = lines.shape[0] // lax.axis_size("shot")
    result = lax.dynamic_slice_in_dim(lines, lax.axis_index("shot") * share, share, 0)
    return (result, prev[None], cur[None])


MESH = pl.DeviceIdType.MESH
F32 = jnp.float32
BF16 = jnp.bfloat16


def split(value):
    high = value.astype(BF16)
    return high, (value - high.astype(F32)).astype(BF16)


def dot(a, b, dims=((1,), (0,))):
    return lax.dot_general(a, b, (dims, ((), ())), preferred_element_type=F32)


def dot3(a, b, dims=((1,), (0,))):
    (ah, al), (bh, bl) = a, b
    return dot(ah, bh, dims) + (dot(ah, bl, dims) + dot(al, bh, dims))


def fused_kernel(
    shots, subs,
    courant, lam_prev, lam_cur, accel, traces, receivers, sources, smooth_x, smooth_y, smooth_z,
    final, fa, fb,
    co, ac, tr, rc, so, sx, sy, sz,
    inj, wts, img, syp, stage, gathered, turned, turned_edge, lines, lines_edge, held, ready,
    local_sem, halo_send, halo_recv, rs_send, rs_recv, aa_send, aa_recv, fin_send, fin_recv,
):
    shot = lax.axis_index("shot")
    sub = lax.axis_index("sub")
    rows, ny, nz = courant.shape
    nx = smooth_x.shape[0]
    halo = STEPS
    ys = ny // shots
    part = ys // subs
    share = nx // shots
    cuts = list(range(halo, rows - halo + 1, halo))
    groups = len(cuts) - 1
    deep = rows - 2 * halo
    inner = subs * deep

    def load(k, src, dst):
        copy = pltpu.make_async_copy(src, dst, local_sem.at[k])
        copy.start()
        return copy

    own = pl.ds(halo, rows)
    loads = [
        load(0, receivers, rc),
        load(1, traces.at[0], tr),
        load(2, sources, so),
        load(3, lam_cur.at[0], fa.at[own]),
        load(4, lam_prev.at[0], fb.at[own]),
        load(5, courant, co.at[own]),
        load(6, accel.at[0], ac),
        load(7, smooth_y, sy),
        load(8, smooth_x, sx),
        load(9, smooth_z, sz),
    ]

    barrier = pltpu.get_barrier_semaphore()
    for d in range(1, subs):
        pl.semaphore_signal(barrier, inc=1, device_id=(shot, lax.rem(sub + d, subs)), device_id_type=MESH)
    for d in range(1, shots):
        pl.semaphore_signal(barrier, inc=1, device_id=(lax.rem(shot + d, shots), sub), device_id_type=MESH)
    loads[0].wait()
    loads[1].wait()
    loads[2].wait()
    rec = rc[...]
    place = (rec[0] - (sub * rows - halo)) * ny + rec[1]
    count = rec.shape[2]
    level = jnp.transpose(jnp.broadcast_to(rec[2], (8, count)))
    depth = level[:, 0:1] == lax.broadcasted_iota(jnp.int32, (count, nz), 1)
    columns = jnp.transpose(tr[...])
    for k in range(STEPS):
        weight = jnp.where(depth, columns[:, k : k + 1], 0.0)
        high, low = split(weight)
        wts[0, :, k * nz : (k + 1) * nz] = high
        wts[1, :, k * nz : (k + 1) * nz] = low
    group = 4
    tall = group * ny

    def inject_rows(g, carry):
        cells = lax.broadcasted_iota(jnp.int32, (tall, count), 0) + g * tall
        hit = jnp.where(cells == place, 1.0, 0.0).astype(BF16)
        for k in range(0, STEPS, 2):
            cut = pl.ds(k * nz, 2 * nz)
            added = dot(hit, wts[0, :, cut]) + dot(hit, wts[1, :, cut])
            for h in range(2):
                inj[k + h, pl.ds(g * group, group)] = added[:, h * nz : (h + 1) * nz].reshape(group, ny, nz)
        return carry

    def inject_until(done, row):
        end = min(-(-(row + halo) // group), (rows + 2 * halo) // group)
        if end > done:
            lax.fori_loop(done, end, inject_rows, 0)
        return max(done, end)

    injected = inject_until((halo + 1) // group, cuts[1] + halo - 1)

    loads[7].wait()
    at = lax.broadcasted_iota(jnp.int32, (ny, ny), 0)
    piece = at // ys
    inside = at - piece * ys
    group_of = inside // part
    origin = group_of * (shots * part) + piece * part + (inside - group_of * part)
    pick = jnp.where(origin == lax.broadcasted_iota(jnp.int32, (ny, ny), 1), 1.0, 0.0).astype(BF16)
    high, low = split(sy[...])
    high = dot(pick, high).astype(BF16)
    low = dot(pick, low).astype(BF16)
    syp[...] = jnp.concatenate([high, high, low], axis=1)

    pl.semaphore_wait(barrier, subs + shots - 2)

    def halo_copies(side):
        target = sub - 1 if side == 0 else sub + 1
        out = []
        for k, (src, dst, width) in enumerate(
            ((lam_cur.at[0], fa, halo), (lam_prev.at[0], fb, halo - 1), (courant, co, halo - 1))
        ):
            if side == 0:
                start, place = 0, halo + rows
            else:
                start, place = rows - width, halo - width
            out.append(pltpu.make_async_remote_copy(
                src_ref=src.at[pl.ds(start, width)],
                dst_ref=dst.at[pl.ds(place, width)],
                send_sem=halo_send.at[side, k],
                recv_sem=halo_recv.at[side, k],
                device_id=(shot, target),
                device_id_type=MESH,
            ))
        return out

    low_side = halo_copies(0)
    high_side = halo_copies(1)

    @pl.when(sub > 0)
    def _():
        for copy in low_side:
            copy.start()

    @pl.when(sub < subs - 1)
    def _():
        for copy in high_side:
            copy.start()

    @pl.when(sub == 0)
    def _():
        for ref in (fa, fb, co):
            ref[pl.ds(0, halo)] = jnp.zeros((halo, ny, nz), F32)

    @pl.when(sub == subs - 1)
    def _():
        for ref in (fa, fb, co):
            ref[pl.ds(halo + rows, halo)] = jnp.zeros((halo, ny, nz), F32)

    yi = lax.broadcasted_iota(jnp.int32, (ny, nz), 0)
    zi = lax.broadcasted_iota(jnp.int32, (ny, nz), 1)

    def fresh_row(k, e):
        src, dst = (fa, fb) if k % 2 == 0 else (fb, fa)
        mid = src[e]
        near = src[e - 1] + src[e + 1]
        near = near + jnp.where(yi == 0, 0.0, pltpu.roll(mid, 1, 0))
        near = near + jnp.where(yi == ny - 1, 0.0, pltpu.roll(mid, ny - 1, 0))
        near = near + jnp.where(zi == 0, 0.0, pltpu.roll(mid, 1, 1))
        near = near + jnp.where(zi == nz - 1, 0.0, pltpu.roll(mid, nz - 1, 1))
        speed = co[e]
        value = 2.0 * mid - dst[e] + speed * speed * (near - 6.0 * mid) + inj[k, e]
        dst[e] = value
        return value

    def image_row(k, x, value):
        term = value * ac[k, x].astype(F32)
        img[x] = term if k == 0 else img[x] + term

    sx0 = so[0, 0].astype(F32)
    dy = yi.astype(F32) - so[0, 1].astype(F32)
    dz = zi.astype(F32) - so[0, 2].astype(F32)
    flat = dy * dy + dz * dz

    def smooth_pair(x):
        planes = []
        for p in range(2):
            dx = (sub * rows + x + p).astype(F32) - sx0
            taper = 1.0 - jnp.exp(-(dx * dx + flat) / float(TAPER * TAPER))
            planes.append(img[x + p] * taper)
        high, low = split(jnp.concatenate(planes, axis=1))
        out = dot(syp[...], jnp.concatenate([high, low, high], axis=0))
        for p in range(2):
            for s in range(shots):
                stage[s, pl.ds(pl.multiple_of((x + p) * ys, ys), ys), :] = out[s * ys : (s + 1) * ys, p * nz : (p + 1) * nz]

    def rs_copy(d, g):
        start, length = (cuts[g] if g < groups else (g - groups) * (rows - halo), halo)
        peer = lax.rem(shot + d, shots)
        cut = pl.ds(start * ys, length * ys)
        return pltpu.make_async_remote_copy(
            src_ref=stage.at[peer, cut],
            dst_ref=gathered.at[d - 1, cut],
            send_sem=rs_send.at[d - 1, g],
            recv_sem=rs_recv.at[d - 1, g],
            device_id=(peer, sub),
            device_id_type=MESH,
        )

    for copy in loads[3:7]:
        copy.wait()
    sends = []
    for g in range(groups):
        final_group = g == groups - 1
        injected = inject_until(injected, rows + halo if final_group else cuts[g + 1] + halo - 1)
        if final_group and (halo + 1) // group > 0:
            lax.fori_loop(0, (halo + 1) // group, inject_rows, 0)
        for k in range(STEPS):
            def body(x, carry, k=k):
                image_row(k, x, fresh_row(k, x + halo))
                return carry

            start = cuts[g] + halo - 1 - k if g else k + 1
            end = rows - 1 - k if final_group else cuts[g + 1] + halo - 1 - k
            lax.fori_loop(start, end, body, 0, unroll=2)

        def pair_body(i, carry, g=g):
            smooth_pair(cuts[g] + 2 * i)
            return carry

        lax.fori_loop(0, halo // 2, pair_body, 0, unroll=2)
        for d in range(1, shots):
            copy = rs_copy(d, g)
            copy.start()
            sends.append(copy)

    @pl.when(sub > 0)
    def _():
        for copy in high_side:
            copy.wait_recv()
        for copy in low_side:
            copy.wait_send()

    @pl.when(sub < subs - 1)
    def _():
        for copy in low_side:
            copy.wait_recv()
        for copy in high_side:
            copy.wait_send()

    for k in range(STEPS):
        for x in list(range(k + 1 - halo, k + 1)) + list(range(rows - 1 - k, rows - 1 - k + halo)):
            value = fresh_row(k, x + halo)
            if 0 <= x < rows:
                image_row(k, x, value)
    for g, start in ((groups, 0), (groups + 1, rows - halo)):
        for i in range(halo // 2):
            smooth_pair(jnp.int32(start + 2 * i))
        for d in range(1, shots):
            copy = rs_copy(d, g)
            copy.start()
            sends.append(copy)

    loads[8].wait()
    loads[9].wait()
    at = lax.broadcasted_iota(jnp.int32, (nx, nx), 1)
    block = at // deep
    middle = block * rows + halo + (at - block * deep)
    past = at - inner
    block = past // (2 * halo)
    offset = past - block * (2 * halo)
    outer = block * rows + jnp.where(offset < halo, offset, offset + deep)
    origin = jnp.where(at < inner, middle, outer)
    pick = jnp.where(origin == lax.broadcasted_iota(jnp.int32, (nx, nx), 0), 1.0, 0.0).astype(BF16)
    sxs = [dot(piece, pick).astype(BF16) for piece in split(sx[...])]
    szs = split(sz[...])

    def gather(r, start, length):
        cut = pl.ds(start * ys + r, length, stride=ys)
        total = stage[shot, cut, :]
        for d in range(1, shots):
            total = total + gathered[d - 1, cut, :]
        return total

    def aa_copy(d, g):
        peer = lax.rem(sub + d, subs)
        src, dst, width = ((turned, lines, deep), (turned_edge, lines_edge, 2 * halo))[g]
        return pltpu.make_async_remote_copy(
            src_ref=src.at[pl.ds(peer * part, part)],
            dst_ref=dst.at[:, pl.ds(pl.multiple_of(sub * width, 8), width), :],
            send_sem=aa_send.at[d - 1, g],
            recv_sem=aa_recv.at[d - 1, g],
            device_id=(shot, peer),
            device_id_type=MESH,
        )

    for copy in sends[: groups * (shots - 1)]:
        copy.wait_recv()
    for r in range(ys):
        turned[r] = gather(r, halo, deep)
    crossing = [aa_copy(d, 0) for d in range(1, subs)]
    for copy in crossing:
        copy.start()
    lines[:, pl.ds(pl.multiple_of(sub * deep, 8), deep), :] = turned[pl.ds(sub * part, part)]
    for copy in sends[groups * (shots - 1) :]:
        copy.wait_recv()
    for r in range(ys):
        turned_edge[r, :halo] = gather(r, 0, halo)
        turned_edge[r, halo:] = gather(r, rows - halo, halo)
    crossing_edge = [aa_copy(d, 1) for d in range(1, subs)]
    for copy in crossing_edge:
        copy.start()
    mine = pl.ds(pl.multiple_of(sub * (2 * halo), 8), 2 * halo)
    lines_edge[:, mine, :] = turned_edge[pl.ds(sub * part, part)]

    for copy in crossing:
        copy.wait_recv()
    for p in range(part):
        held[p] = dot3([piece[:, :inner] for piece in sxs], split(lines[p]))
    for copy in crossing_edge:
        copy.wait_recv()

    def fin_copy(d, p):
        peer = lax.rem(shot + d, shots)
        return pltpu.make_async_remote_copy(
            src_ref=ready.at[peer, p],
            dst_ref=final.at[shot, p],
            send_sem=fin_send.at[d - 1, p],
            recv_sem=fin_recv.at[d - 1, p],
            device_id=(peer, sub),
            device_id_type=MESH,
        )

    last = []
    for p in range(part):
        value = held[p] + dot3([piece[:, inner:] for piece in sxs], split(lines_edge[p]))
        value = dot3(split(value), szs, ((1,), (1,)))
        ready[:, p] = value.reshape(shots, share, nz)
        for d in range(1, shots):
            copy = fin_copy(d, p)
            copy.start()
            last.append(copy)
    final[shot] = ready[shot]
    for copy in last:
        copy.wait_recv()
    for copy in sends + crossing + crossing_edge + last:
        copy.wait_send()


def place_kernel(pieces, newer, older, grad, prev_out, cur_out, outv, store_sem):
    rows = prev_out.shape[1]
    own = pl.ds((newer.shape[0] - rows) // 2, rows)
    stores = [
        pltpu.make_async_copy(older.at[own], prev_out.at[0], store_sem.at[0]),
        pltpu.make_async_copy(newer.at[own], cur_out.at[0], store_sem.at[1]),
    ]
    for copy in stores:
        copy.start()
    shots, part, share, _ = pieces.shape
    for s in range(shots):
        for p in range(part):
            outv[pl.ds(s * part + p, share, stride=shots * part), :] = pieces[s, p]
    put = pltpu.make_async_copy(outv, grad, store_sem.at[2])
    put.start()
    for copy in stores + [put]:
        copy.wait()


def fused(shots, subs, *args):
    courant, lam_prev, _, accel, traces, receivers, sources, smooth_x, smooth_y, smooth_z = args
    rows, ny, nz = courant.shape
    nx = smooth_x.shape[0]
    ys = ny // shots
    part = ys // subs
    share = nx // shots
    tall = rows + 2 * STEPS
    field = lam_prev.shape
    receivers = jnp.transpose(receivers, (2, 0, 1))
    args = args[:5] + (receivers,) + args[6:]
    anywhere = pl.BlockSpec(memory_space=pltpu.HBM)
    dma = pltpu.SemaphoreType.DMA
    vmem = pl.BlockSpec(memory_space=pltpu.VMEM)
    grad, newer, older = pl.pallas_call(
        functools.partial(fused_kernel, shots, subs),
        out_shape=(
            pltpu.VMEM((shots, part, share, nz), F32),
            pltpu.VMEM((tall, ny, nz), F32),
            pltpu.VMEM((tall, ny, nz), F32),
        ),
        in_specs=[anywhere] * len(args),
        out_specs=(vmem,) * 3,
        scratch_shapes=[
            pltpu.VMEM((tall, ny, nz), F32),
            pltpu.VMEM(accel.shape[1:], accel.dtype),
            pltpu.VMEM(traces.shape[1:], F32),
            pltpu.VMEM(receivers.shape, jnp.int32),
            pltpu.SMEM(sources.shape, jnp.int32),
            pltpu.VMEM(smooth_x.shape, F32),
            pltpu.VMEM(smooth_y.shape, F32),
            pltpu.VMEM(smooth_z.shape, F32),
            pltpu.VMEM((STEPS, tall, ny, nz), F32),
            pltpu.VMEM((2, receivers.shape[2], STEPS * nz), BF16),
            pltpu.VMEM((rows, ny, nz), F32),
            pltpu.VMEM((ny, 3 * ny), BF16),
            pltpu.VMEM((shots, rows * ys, nz), F32),
            pltpu.VMEM((shots - 1, rows * ys, nz), F32),
            pltpu.VMEM((ys, rows - 2 * STEPS, nz), F32),
            pltpu.VMEM((ys, 2 * STEPS, nz), F32),
            pltpu.VMEM((part, subs * (rows - 2 * STEPS), nz), F32),
            pltpu.VMEM((part, subs * 2 * STEPS, nz), F32),
            pltpu.VMEM((part, nx, nz), F32),
            pltpu.VMEM((shots, part, share, nz), F32),
            dma((10,)),
            dma((2, 3)),
            dma((2, 3)),
            dma((shots - 1, rows // STEPS)),
            dma((shots - 1, rows // STEPS)),
            dma((subs - 1, 2)),
            dma((subs - 1, 2)),
            dma((shots - 1, part)),
            dma((shots - 1, part)),
        ],
        compiler_params=pltpu.CompilerParams(
            collective_id=0, has_side_effects=True, vmem_limit_bytes=67043328 - 4 * (2 * tall * ny * nz + 2 * shots * part * share * nz)
        ),
    )(*args)
    grad, prev_out, cur_out = pl.pallas_call(
        place_kernel,
        out_shape=(
            jax.ShapeDtypeStruct((share * shots * part, nz), F32),
            jax.ShapeDtypeStruct(field, F32),
            jax.ShapeDtypeStruct(field, F32),
        ),
        in_specs=[vmem] * 3,
        out_specs=(anywhere,) * 3,
        scratch_shapes=[
            pltpu.VMEM((share * shots * part, nz), F32),
            dma((3,)),
        ],
        compiler_params=pltpu.CompilerParams(vmem_limit_bytes=8 * 2**20),
    )(grad, newer, older)
    return (grad.reshape(share, shots * part, nz), prev_out, cur_out)


def solution(mesh):
    in_specs = (
        P("sub", None, None),
        P("shot", "sub", None, None),
        P("shot", "sub", None, None),
        P("shot", None, "sub", None, None),
        P("shot", None, None),
        P("shot", None, None),
        P("shot", None),
        P(),
        P(),
        P(),
    )
    out_specs = (P("shot", "sub", None), P("shot", "sub", None, None), P("shot", "sub", None, None))
    shots, subs = mesh.shape["shot"], mesh.shape["sub"]

    def run(*args):
        courant, smooth_x, receivers = args[0], args[7], args[5]
        rows, ny, nz = courant.shape
        fits = (
            ny % (8 * shots) == 0
            and ny % (shots * subs) == 0
            and rows % 8 == 0
            and rows > 2 * STEPS
            and rows % 12 == 0
            and smooth_x.shape[0] % (8 * shots) == 0
            and nz % 128 == 0
            and shots > 1
            and subs > 1
        )
        return fused(shots, subs, *args) if fits else shards(*args)

    return jax.shard_map(run, mesh=mesh, in_specs=in_specs, out_specs=out_specs, check_vma=False)
```

```python
import functools

import jax
import jax.numpy as jnp
from jax import lax
from jax.experimental import pallas as pl
from jax.experimental.pallas import tpu as pltpu
from jax.sharding import PartitionSpec as P

STEPS = 4
TAPER = 8


def with_halo(value, sides, width):
    for axis, dim in sides:
        count, length = (lax.axis_size(axis), value.shape[dim])
        up = [(i, (i + 1) % count) for i in range(count - 1)]
        down = [(j, i) for i, j in up]
        last = lax.slice_in_dim(value, length - width, length, axis=dim)
        initial = lax.slice_in_dim(value, 0, width, axis=dim)
        before = lax.ppermute(last, axis, up)
        after = lax.ppermute(initial, axis, down)
        value = jnp.concatenate([before, value, after], axis=dim)
    return value


def plane_sum(block):
    side = jnp.pad(block, ((0, 0), (1, 1), (1, 1)))
    total = side[:, 2:, 1:-1] + side[:, :-2, 1:-1]
    return total + side[:, 1:-1, 2:] + side[:, 1:-1, :-2]


def inject(group_rec, weights, start, length, width_y, width_z):
    row_hit = (group_rec[None, :, 0] - start == jnp.arange(length)[:, None]).astype(jnp.float32)
    col_hit = (group_rec[None, :, 1] == jnp.arange(width_y)[:, None]).astype(jnp.float32)
    depth_hit = (group_rec[None, :, 2] == jnp.arange(width_z)[:, None]).astype(jnp.float32)
    plane = row_hit[:, None, :] * col_hit[None, :, :]
    depth_weight = depth_hit * weights[None, :]
    return jnp.einsum("abr,cr->abc", plane, depth_weight, precision=lax.Precision.HIGHEST)


def shards(
    courant, lam_prev, lam_cur, accel, traces, receivers, sources, smooth_x, smooth_y, smooth_z
):
    rows = courant.shape[0]
    width_y = courant.shape[1]
    width_z = courant.shape[2]
    first = lax.axis_index("sub") * rows
    coeff = courant * courant
    prev = lam_prev[0]
    cur = lam_cur[0]
    group_rec = receivers[0]
    image = jnp.zeros_like(cur)
    for step in range(STEPS):
        padded = with_halo(cur, (("sub", 0),), 1)
        beside = padded[2:] + padded[:-2] + plane_sum(cur)
        fresh = 2.0 * cur - prev + coeff * (beside - 6.0 * cur)
        fresh = fresh + inject(group_rec, traces[0, step], first, rows, width_y, width_z)
        image = image + fresh * accel[0, step].astype(jnp.float32)
        prev, cur = (cur, fresh)
    source = sources[0].astype(jnp.float32)
    xpos = (first + jnp.arange(rows)).astype(jnp.float32)[:, None, None]
    ypos = jnp.arange(width_y).astype(jnp.float32)[None, :, None]
    zpos = jnp.arange(width_z).astype(jnp.float32)[None, None, :]
    dist = (xpos - source[0]) ** 2 + (ypos - source[1]) ** 2 + (zpos - source[2]) ** 2
    image = image * (1.0 - jnp.exp(-dist / float(TAPER * TAPER)))
    high = lax.Precision.HIGHEST
    total = lax.psum(image, "shot")
    total = jnp.einsum("abc,kc->abk", total, smooth_z, precision=high)
    total = jnp.einsum("abk,jb->ajk", total, smooth_y, precision=high)
    lines = lax.all_to_all(total, "sub", split_axis=1, concat_axis=0, tiled=True)
    lines = jnp.einsum("ajk,ia->ijk", lines, smooth_x, precision=high)
    share = lines.shape[0] // lax.axis_size("shot")
    result = lax.dynamic_slice_in_dim(lines, lax.axis_index("shot") * share, share, 0)
    return (result, prev[None], cur[None])


MESH = pl.DeviceIdType.MESH
F32 = jnp.float32
BF16 = jnp.bfloat16


def split(value):
    high = value.astype(BF16)
    return high, (value - high.astype(F32)).astype(BF16)


def dot(a, b, dims=((1,), (0,))):
    return lax.dot_general(a, b, (dims, ((), ())), preferred_element_type=F32)


def dot3(a, b, dims=((1,), (0,))):
    (ah, al), (bh, bl) = a, b
    return dot(ah, bh, dims) + (dot(ah, bl, dims) + dot(al, bh, dims))


def stack3(value, axis):
    high, low = split(value)
    return jnp.concatenate([high, low, high], axis=axis)


def fused_kernel(
    shots, subs,
    courant, lam_prev, lam_cur, accel, traces, receivers, sources, smooth_x, smooth_y, smooth_z,
    final, fa, fb,
    co, ac, tr, rc, so, sx, sy, sz,
    inj, wts, img, syp, sxp, szp, stage, gathered, turned, lines, held, ready,
    local_sem, halo_send, halo_recv, rs_send, rs_recv, aa_send, aa_recv, fin_send, fin_recv,
):
    shot = lax.axis_index("shot")
    sub = lax.axis_index("sub")
    rows, ny, nz = courant.shape
    nx = smooth_x.shape[0]
    halo = STEPS
    ys = ny // shots
    part = ys // subs
    share = nx // shots
    cuts = list(range(halo, rows - halo + 1, halo))
    groups = len(cuts) - 1
    deep = rows - 2 * halo
    wide = 2 * halo
    blocks = rows // wide
    early = cuts[1] + halo

    def load(k, src, dst):
        copy = pltpu.make_async_copy(src, dst, local_sem.at[k])
        copy.start()
        return copy

    def pieces(k, start, length):
        here, there = pl.ds(start, length), pl.ds(halo + start, length)
        return [
            load(k, lam_cur.at[0, here], fa.at[there]),
            load(k + 1, lam_prev.at[0, here], fb.at[there]),
            load(k + 2, courant.at[here], co.at[there]),
            load(k + 3, accel.at[0, :, here], ac.at[:, here]),
        ]

    loads = [load(0, receivers, rc), load(1, traces.at[0], tr), load(2, sources, so)]
    first_rows = pieces(3, 0, early)
    loads.append(load(11, smooth_y, sy))
    other_rows = pieces(7, early, rows - early)
    loads += [load(12, smooth_x, sx), load(13, smooth_z, sz)]

    if shots == 4:
        peers = [3 - shot, shot + 1 - 2 * lax.rem(shot, 2), lax.rem(shot + 2, 4)]
    else:
        peers = [lax.rem(shot + d, shots) for d in range(1, shots)]

    barrier = pltpu.get_barrier_semaphore()
    for d in range(1, subs):
        pl.semaphore_signal(barrier, inc=1, device_id=(shot, lax.rem(sub + d, subs)), device_id_type=MESH)
    for peer in peers:
        pl.semaphore_signal(barrier, inc=1, device_id=(peer, sub), device_id_type=MESH)
    loads[0].wait()
    loads[1].wait()
    loads[2].wait()
    rec = rc[...]
    place = (rec[0] - (sub * rows - halo)) * ny + rec[1]
    count = rec.shape[2]
    level = jnp.transpose(jnp.broadcast_to(rec[2], (8, count)))
    depth = level[:, 0:1] == lax.broadcasted_iota(jnp.int32, (count, nz), 1)
    columns = jnp.transpose(tr[...])
    for k in range(STEPS):
        weight = jnp.where(depth, columns[:, k : k + 1], 0.0)
        high, low = split(weight)
        wts[0, :, k * nz : (k + 1) * nz] = high
        wts[1, :, k * nz : (k + 1) * nz] = low
    group = 4
    tall = group * ny

    def inject_rows(g, carry):
        cells = lax.broadcasted_iota(jnp.int32, (tall, count), 0) + g * tall
        hit = jnp.where(cells == place, 1.0, 0.0).astype(BF16)
        for k in range(0, STEPS, 2):
            cut = pl.ds(k * nz, 2 * nz)
            added = dot(hit, wts[0, :, cut]) + dot(hit, wts[1, :, cut])
            for h in range(2):
                inj[k + h, pl.ds(g * group, group)] = added[:, h * nz : (h + 1) * nz].reshape(group, ny, nz)
        return carry

    def inject_until(done, row):
        end = min(-(-(row + halo) // group), (rows + 2 * halo) // group)
        if end > done:
            lax.fori_loop(done, end, inject_rows, 0)
        return max(done, end)

    injected = inject_until((halo + 1) // group, cuts[1] + halo - 1)

    loads[3].wait()
    at = lax.broadcasted_iota(jnp.int32, (ny, ny), 0)
    piece = at // ys
    inside = at - piece * ys
    side = inside // subs
    origin = (inside - side * subs) * (shots * part) + piece * part + side
    pick = jnp.where(origin == lax.broadcasted_iota(jnp.int32, (ny, ny), 1), 1.0, 0.0).astype(BF16)
    high, low = split(sy[...])
    high = dot(pick, high).astype(BF16)
    low = dot(pick, low).astype(BF16)
    syp[...] = jnp.concatenate([high, high, low], axis=1)

    pl.semaphore_wait(barrier, subs + shots - 2)

    def halo_copies(side):
        target = sub - 1 if side == 0 else sub + 1
        out = []
        for k, (src, dst, width) in enumerate(
            ((lam_cur.at[0], fa, halo), (lam_prev.at[0], fb, halo - 1), (courant, co, halo - 1))
        ):
            if side == 0:
                start, place = 0, halo + rows
            else:
                start, place = rows - width, halo - width
            out.append(pltpu.make_async_remote_copy(
                src_ref=src.at[pl.ds(start, width)],
                dst_ref=dst.at[pl.ds(place, width)],
                send_sem=halo_send.at[side, k],
                recv_sem=halo_recv.at[side, k],
                device_id=(shot, target),
                device_id_type=MESH,
            ))
        return out

    low_side = halo_copies(0)
    high_side = halo_copies(1)

    @pl.when(sub > 0)
    def _():
        for copy in low_side:
            copy.start()

    @pl.when(sub < subs - 1)
    def _():
        for copy in high_side:
            copy.start()

    @pl.when(sub == 0)
    def _():
        for ref in (fa, fb, co):
            ref[pl.ds(0, halo)] = jnp.zeros((halo, ny, nz), F32)

    @pl.when(sub == subs - 1)
    def _():
        for ref in (fa, fb, co):
            ref[pl.ds(halo + rows, halo)] = jnp.zeros((halo, ny, nz), F32)

    yi = lax.broadcasted_iota(jnp.int32, (ny, nz), 0)
    zi = lax.broadcasted_iota(jnp.int32, (ny, nz), 1)

    def fresh_row(k, e):
        src, dst = (fa, fb) if k % 2 == 0 else (fb, fa)
        mid = src[e]
        near = src[e - 1] + src[e + 1]
        near = near + jnp.where(yi == 0, 0.0, pltpu.roll(mid, 1, 0))
        near = near + jnp.where(yi == ny - 1, 0.0, pltpu.roll(mid, ny - 1, 0))
        near = near + jnp.where(zi == 0, 0.0, pltpu.roll(mid, 1, 1))
        near = near + jnp.where(zi == nz - 1, 0.0, pltpu.roll(mid, nz - 1, 1))
        speed = co[e]
        value = 2.0 * mid - dst[e] + speed * speed * (near - 6.0 * mid) + inj[k, e]
        dst[e] = value
        return value

    def image_row(k, x, value):
        term = value * ac[k, x].astype(F32)
        img[x] = term if k == 0 else img[x] + term

    sx0 = so[0, 0].astype(F32)
    dy = yi.astype(F32) - so[0, 1].astype(F32)
    dz = zi.astype(F32) - so[0, 2].astype(F32)
    flat = dy * dy + dz * dz

    def smooth_pair(x):
        planes = []
        for p in range(2):
            dx = (sub * rows + (x + p)).astype(F32) - sx0
            taper = 1.0 - jnp.exp(-(dx * dx + flat) / float(TAPER * TAPER))
            planes.append(img[x + p] * taper)
        out = dot(syp[...], stack3(jnp.concatenate(planes, axis=1), 0))
        for q in range(2):
            spot = pl.ds(slot(x + q) * subs, subs)
            for s in range(shots):
                for p in range(part):
                    at = s * ys + p * subs
                    stage[s, p, spot, :] = out[at : at + subs, q * nz : (q + 1) * nz]

    def slot(x):
        return x - halo if halo <= x < rows - halo else x + deep if x < halo else x

    def rs_copies(g):
        if g < groups:
            side, cut = slice(None), pl.ds(slot(cuts[g]) * subs, halo * subs)
        else:
            side, cut = g - groups, pl.ds(deep * subs, wide * subs)
        return [
            pltpu.make_async_remote_copy(
                src_ref=stage.at[peer, side, cut],
                dst_ref=gathered.at[d, side, cut],
                send_sem=rs_send.at[d, g],
                recv_sem=rs_recv.at[d, g],
                device_id=(peer, sub),
                device_id_type=MESH,
            )
            for d, peer in enumerate(peers)
        ]

    for copy in first_rows:
        copy.wait()
    sends = []
    for g in range(groups):
        if g == 1:
            for copy in other_rows:
                copy.wait()
        final_group = g == groups - 1
        injected = inject_until(injected, rows + halo if final_group else cuts[g + 1] + halo - 1)
        if final_group and (halo + 1) // group > 0:
            lax.fori_loop(0, (halo + 1) // group, inject_rows, 0)
        for k in range(STEPS):
            start = cuts[g] + halo - 1 - k if g else k + 1
            end = rows - 1 - k if final_group else cuts[g + 1] + halo - 1 - k
            for x in range(start, end):
                image_row(k, x, fresh_row(k, x + halo))

        for i in range(halo // 2):
            smooth_pair(cuts[g] + 2 * i)
        sends.append(rs_copies(g))
        for copy in sends[g]:
            copy.start()

    @pl.when(sub > 0)
    def _():
        for copy in high_side:
            copy.wait_recv()
        for copy in low_side:
            copy.wait_send()

    @pl.when(sub < subs - 1)
    def _():
        for copy in low_side:
            copy.wait_recv()
        for copy in high_side:
            copy.wait_send()

    for k in range(STEPS):
        for x in list(range(k + 1 - halo, k + 1)) + list(range(rows - 1 - k, rows - 1 - k + halo)):
            value = fresh_row(k, x + halo)
            if 0 <= x < rows:
                image_row(k, x, value)
    for x in list(range(0, halo, 2)) + list(range(rows - halo, rows, 2)):
        smooth_pair(x)
    for p in range(part):
        sends.append(rs_copies(groups + p))
        for copy in sends[groups + p]:
            copy.start()

    loads[4].wait()
    loads[5].wait()
    at = lax.broadcasted_iota(jnp.int32, (nx, 3 * nx), 1)
    block = at // (3 * subs * wide)
    place = at - block * (3 * subs * wide)
    term = place // (subs * wide)
    place = place - term * (subs * wide)
    where = place // wide
    place = place - where * wide
    edge = jnp.where(place < halo, place, place + deep)
    origin = where * rows + jnp.where(block < blocks - 1, halo + block * wide + place, edge)
    pick = jnp.where(origin == lax.broadcasted_iota(jnp.int32, (nx, 3 * nx), 0), 1.0, 0.0)
    high, low = split(sx[...])
    high = dot(high, jnp.where(term < 2, pick, 0.0).astype(BF16))
    low = dot(low, jnp.where(term < 2, 0.0, pick).astype(BF16))
    sxp[...] = (high + low).astype(BF16)
    high, low = split(jnp.transpose(sz[...]))
    szp[...] = jnp.concatenate([high, high, low], axis=0)

    def gather(b, p):
        for u in range(subs):
            cut = pl.ds(b * wide * subs + u, wide, stride=subs)
            total = stage[shot, p, cut, :]
            for d in range(shots - 1):
                total = total + gathered[d, p, cut, :]
            turned[b, p, u] = total

    def aa_copies(g):
        b, side = (g, slice(None)) if g < blocks - 1 else (blocks - 1, g - blocks + 1)
        spot = pl.ds(pl.multiple_of(sub * wide, 8), wide)
        out = []
        for d in range(1, subs):
            peer = lax.rem(sub + d, subs)
            out.append(pltpu.make_async_remote_copy(
                src_ref=turned.at[b, side, peer],
                dst_ref=lines.at[b, side, spot],
                send_sem=aa_send.at[d - 1, g],
                recv_sem=aa_recv.at[d - 1, g],
                device_id=(shot, peer),
                device_id_type=MESH,
            ))
        return out

    def keep(b, p):
        lines[b, p, pl.ds(pl.multiple_of(sub * wide, 8), wide), :] = turned[b, p, sub]

    def product(b, p):
        span = 3 * subs * wide
        return dot(sxp[:, b * span : (b + 1) * span], stack3(lines[b, p], 0))

    crossing = []
    for b in range(blocks - 1):
        for copies in sends[2 * b : 2 * b + 2]:
            for copy in copies:
                copy.wait_recv()
        for p in range(part):
            gather(b, p)
        crossing.append(aa_copies(b))
        for copy in crossing[b]:
            copy.start()
        for p in range(part):
            keep(b, p)
    for p in range(part):
        for copy in sends[groups + p]:
            copy.wait_recv()
        gather(blocks - 1, p)
        crossing.append(aa_copies(blocks - 1 + p))
        for copy in crossing[blocks - 1 + p]:
            copy.start()
        keep(blocks - 1, p)

    for b in range(blocks - 1):
        for copy in crossing[b]:
            copy.wait_recv()
        for p in range(part):
            value = product(b, p)
            held[p] = value if b == 0 else held[p] + value

    last = []
    for p in range(part):
        for copy in crossing[blocks - 1 + p]:
            copy.wait_recv()
        value = held[p] + product(blocks - 1, p)
        value = dot(stack3(value, 1), szp[...])
        ready[:, p] = value.reshape(shots, share, nz)
        for d, peer in enumerate(peers):
            copy = pltpu.make_async_remote_copy(
                src_ref=ready.at[peer, p],
                dst_ref=final.at[shot, p],
                send_sem=fin_send.at[d, p],
                recv_sem=fin_recv.at[d, p],
                device_id=(peer, sub),
                device_id_type=MESH,
            )
            copy.start()
            last.append(copy)
    final[shot] = ready[shot]
    for copies in sends + crossing:
        for copy in copies:
            copy.wait_send()
    for copy in last:
        copy.wait()


def place_kernel(pieces, newer, older, grad, prev_out, cur_out, outv, store_sem):
    rows = prev_out.shape[1]
    own = pl.ds((newer.shape[0] - rows) // 2, rows)
    stores = [
        pltpu.make_async_copy(older.at[own], prev_out.at[0], store_sem.at[0]),
        pltpu.make_async_copy(newer.at[own], cur_out.at[0], store_sem.at[1]),
    ]
    for copy in stores:
        copy.start()
    shots, part, share, _ = pieces.shape
    for s in range(shots):
        for p in range(part):
            outv[pl.ds(s * part + p, share, stride=shots * part), :] = pieces[s, p]
    put = pltpu.make_async_copy(outv, grad, store_sem.at[2])
    put.start()
    for copy in stores + [put]:
        copy.wait()


def fused(shots, subs, *args):
    courant, lam_prev, _, accel, traces, receivers, sources, smooth_x, smooth_y, smooth_z = args
    rows, ny, nz = courant.shape
    nx = smooth_x.shape[0]
    ys = ny // shots
    part = ys // subs
    share = nx // shots
    wide = 2 * STEPS
    tall = rows + wide
    blocks = rows // wide
    groups = (rows - wide) // STEPS
    field = lam_prev.shape
    receivers = jnp.transpose(receivers, (2, 0, 1))
    args = args[:5] + (receivers,) + args[6:]
    anywhere = pl.BlockSpec(memory_space=pltpu.HBM)
    dma = pltpu.SemaphoreType.DMA
    vmem = pl.BlockSpec(memory_space=pltpu.VMEM)
    grad, newer, older = pl.pallas_call(
        functools.partial(fused_kernel, shots, subs),
        out_shape=(
            pltpu.VMEM((shots, part, share, nz), F32),
            pltpu.VMEM((tall, ny, nz), F32),
            pltpu.VMEM((tall, ny, nz), F32),
        ),
        in_specs=[anywhere] * len(args),
        out_specs=(vmem,) * 3,
        scratch_shapes=[
            pltpu.VMEM((tall, ny, nz), F32),
            pltpu.VMEM(accel.shape[1:], accel.dtype),
            pltpu.VMEM(traces.shape[1:], F32),
            pltpu.VMEM(receivers.shape, jnp.int32),
            pltpu.SMEM(sources.shape, jnp.int32),
            pltpu.VMEM(smooth_x.shape, F32),
            pltpu.VMEM(smooth_y.shape, F32),
            pltpu.VMEM(smooth_z.shape, F32),
            pltpu.VMEM((STEPS, tall, ny, nz), F32),
            pltpu.VMEM((2, receivers.shape[2], STEPS * nz), BF16),
            pltpu.VMEM((rows, ny, nz), F32),
            pltpu.VMEM((ny, 3 * ny), BF16),
            pltpu.VMEM((nx, 3 * nx), BF16),
            pltpu.VMEM((3 * nz, nz), BF16),
            pltpu.VMEM((shots, part, rows * subs, nz), F32),
            pltpu.VMEM((shots - 1, part, rows * subs, nz), F32),
            pltpu.VMEM((blocks, part, subs, wide, nz), F32),
            pltpu.VMEM((blocks, part, subs * wide, nz), F32),
            pltpu.VMEM((part, nx, nz), F32),
            pltpu.VMEM((shots, part, share, nz), F32),
            dma((14,)),
            dma((2, 3)),
            dma((2, 3)),
            dma((shots - 1, groups + part)),
            dma((shots - 1, groups + part)),
            dma((subs - 1, blocks - 1 + part)),
            dma((subs - 1, blocks - 1 + part)),
            dma((shots - 1, part)),
            dma((shots - 1, part)),
        ],
        compiler_params=pltpu.CompilerParams(
            collective_id=0, has_side_effects=True, vmem_limit_bytes=67043328 - 4 * (2 * tall * ny * nz + 2 * shots * part * share * nz)
        ),
    )(*args)
    grad, prev_out, cur_out = pl.pallas_call(
        place_kernel,
        out_shape=(
            jax.ShapeDtypeStruct((share * shots * part, nz), F32),
            jax.ShapeDtypeStruct(field, F32),
            jax.ShapeDtypeStruct(field, F32),
        ),
        in_specs=[vmem] * 3,
        out_specs=(anywhere,) * 3,
        scratch_shapes=[
            pltpu.VMEM((share * shots * part, nz), F32),
            dma((3,)),
        ],
        compiler_params=pltpu.CompilerParams(vmem_limit_bytes=8 * 2**20),
    )(grad, newer, older)
    return (grad.reshape(share, shots * part, nz), prev_out, cur_out)


def solution(mesh):
    in_specs = (
        P("sub", None, None),
        P("shot", "sub", None, None),
        P("shot", "sub", None, None),
        P("shot", None, "sub", None, None),
        P("shot", None, None),
        P("shot", None, None),
        P("shot", None),
        P(),
        P(),
        P(),
    )
    out_specs = (P("shot", "sub", None), P("shot", "sub", None, None), P("shot", "sub", None, None))
    shots, subs = mesh.shape["shot"], mesh.shape["sub"]

    def run(*args):
        courant, smooth_x, receivers = args[0], args[7], args[5]
        rows, ny, nz = courant.shape
        fits = (
            ny % (8 * shots) == 0
            and ny % (shots * subs) == 0
            and rows % 8 == 0
            and rows > 2 * STEPS
            and subs % 8 == 0
            and smooth_x.shape[0] % (8 * shots) == 0
            and nz % 128 == 0
            and shots > 1
            and subs > 1
        )
        return fused(shots, subs, *args) if fits else shards(*args)

    return jax.shard_map(run, mesh=mesh, in_specs=in_specs, out_specs=out_specs, check_vma=False)
```

```python
import functools

import jax
import jax.numpy as jnp
from jax import lax
from jax.experimental import pallas as pl
from jax.experimental.pallas import tpu as pltpu
from jax.sharding import PartitionSpec as P

STEPS = 4
TAPER = 8


def with_halo(value, sides, width):
    for axis, dim in sides:
        count, length = (lax.axis_size(axis), value.shape[dim])
        up = [(i, (i + 1) % count) for i in range(count - 1)]
        down = [(j, i) for i, j in up]
        last = lax.slice_in_dim(value, length - width, length, axis=dim)
        initial = lax.slice_in_dim(value, 0, width, axis=dim)
        before = lax.ppermute(last, axis, up)
        after = lax.ppermute(initial, axis, down)
        value = jnp.concatenate([before, value, after], axis=dim)
    return value


def plane_sum(block):
    side = jnp.pad(block, ((0, 0), (1, 1), (1, 1)))
    total = side[:, 2:, 1:-1] + side[:, :-2, 1:-1]
    return total + side[:, 1:-1, 2:] + side[:, 1:-1, :-2]


def inject(group_rec, weights, start, length, width_y, width_z):
    row_hit = (group_rec[None, :, 0] - start == jnp.arange(length)[:, None]).astype(jnp.float32)
    col_hit = (group_rec[None, :, 1] == jnp.arange(width_y)[:, None]).astype(jnp.float32)
    depth_hit = (group_rec[None, :, 2] == jnp.arange(width_z)[:, None]).astype(jnp.float32)
    plane = row_hit[:, None, :] * col_hit[None, :, :]
    depth_weight = depth_hit * weights[None, :]
    return jnp.einsum("abr,cr->abc", plane, depth_weight, precision=lax.Precision.HIGHEST)


def shards(
    courant, lam_prev, lam_cur, accel, traces, receivers, sources, smooth_x, smooth_y, smooth_z
):
    rows = courant.shape[0]
    width_y = courant.shape[1]
    width_z = courant.shape[2]
    first = lax.axis_index("sub") * rows
    coeff = courant * courant
    prev = lam_prev[0]
    cur = lam_cur[0]
    group_rec = receivers[0]
    image = jnp.zeros_like(cur)
    for step in range(STEPS):
        padded = with_halo(cur, (("sub", 0),), 1)
        beside = padded[2:] + padded[:-2] + plane_sum(cur)
        fresh = 2.0 * cur - prev + coeff * (beside - 6.0 * cur)
        fresh = fresh + inject(group_rec, traces[0, step], first, rows, width_y, width_z)
        image = image + fresh * accel[0, step].astype(jnp.float32)
        prev, cur = (cur, fresh)
    source = sources[0].astype(jnp.float32)
    xpos = (first + jnp.arange(rows)).astype(jnp.float32)[:, None, None]
    ypos = jnp.arange(width_y).astype(jnp.float32)[None, :, None]
    zpos = jnp.arange(width_z).astype(jnp.float32)[None, None, :]
    dist = (xpos - source[0]) ** 2 + (ypos - source[1]) ** 2 + (zpos - source[2]) ** 2
    image = image * (1.0 - jnp.exp(-dist / float(TAPER * TAPER)))
    high = lax.Precision.HIGHEST
    total = lax.psum(image, "shot")
    total = jnp.einsum("abc,kc->abk", total, smooth_z, precision=high)
    total = jnp.einsum("abk,jb->ajk", total, smooth_y, precision=high)
    lines = lax.all_to_all(total, "sub", split_axis=1, concat_axis=0, tiled=True)
    lines = jnp.einsum("ajk,ia->ijk", lines, smooth_x, precision=high)
    share = lines.shape[0] // lax.axis_size("shot")
    result = lax.dynamic_slice_in_dim(lines, lax.axis_index("shot") * share, share, 0)
    return (result, prev[None], cur[None])


MESH = pl.DeviceIdType.MESH
F32 = jnp.float32
BF16 = jnp.bfloat16


def split(value):
    high = value.astype(BF16)
    return high, (value - high.astype(F32)).astype(BF16)


def dot(a, b, dims=((1,), (0,))):
    return lax.dot_general(a, b, (dims, ((), ())), preferred_element_type=F32)


def dot3(a, b, dims=((1,), (0,))):
    (ah, al), (bh, bl) = a, b
    return dot(ah, bh, dims) + (dot(ah, bl, dims) + dot(al, bh, dims))


CHUNK = 16


def stack3(value, axis):
    high, low = split(value)
    return jnp.concatenate([high, low, high], axis=axis)


def fused_kernel(
    shots, subs,
    courant, lam_prev, lam_cur, accel, traces, receivers, sources, smooth_x, smooth_y, smooth_z,
    final, fa, fb,
    co, ac, tr, rc, so, sx, sy, sz,
    inj, wts, img, syp, sxp, szp, stage, gathered, turned, lines, held, ready,
    local_sem, halo_send, halo_recv, rs_send, rs_recv, aa_send, aa_recv, fin_send, fin_recv,
):
    shot = lax.axis_index("shot")
    sub = lax.axis_index("sub")
    rows, ny, nz = courant.shape
    nx = smooth_x.shape[0]
    halo = STEPS
    ys = ny // shots
    part = ys // subs
    share = nx // shots
    cuts = list(range(halo, rows - halo + 1, halo))
    groups = len(cuts) - 1
    deep = rows - 2 * halo
    wide = 2 * halo
    tall = rows + wide
    blocks = rows // wide
    early = cuts[1] + halo

    def load(k, src, dst):
        copy = pltpu.make_async_copy(src, dst, local_sem.at[k])
        copy.start()
        return copy

    def pieces(k, start, length):
        here, there = pl.ds(start, length), pl.ds(halo + start, length)
        return [
            load(k, lam_cur.at[0, here], fa.at[there]),
            load(k + 1, lam_prev.at[0, here], fb.at[there]),
            load(k + 2, courant.at[here], co.at[there]),
            load(k + 3, accel.at[0, :, here], ac.at[:, here]),
        ]

    loads = [load(0, receivers, rc), load(1, traces.at[0], tr), load(2, sources, so)]
    first_rows = pieces(3, 0, early)
    loads.append(load(11, smooth_y, sy))
    other_rows = pieces(7, early, rows - early)
    loads += [load(12, smooth_x, sx), load(13, smooth_z, sz)]

    if shots == 4:
        peers = [3 - shot, shot + 1 - 2 * lax.rem(shot, 2), lax.rem(shot + 2, 4)]
    else:
        peers = [lax.rem(shot + d, shots) for d in range(1, shots)]

    barrier = pltpu.get_barrier_semaphore()
    for d in range(1, subs):
        pl.semaphore_signal(barrier, inc=1, device_id=(shot, lax.rem(sub + d, subs)), device_id_type=MESH)
    for peer in peers:
        pl.semaphore_signal(barrier, inc=1, device_id=(peer, sub), device_id_type=MESH)
    loads[0].wait()
    loads[1].wait()
    loads[2].wait()
    rec = rc[...]
    place = (rec[0] - (sub * rows - halo)) * ny + rec[1]
    count = rec.shape[2]
    level = jnp.transpose(jnp.broadcast_to(rec[2], (8, count)))
    depth = level[:, 0:1] == lax.broadcasted_iota(jnp.int32, (count, nz), 1)
    columns = jnp.transpose(tr[...])
    for k in range(STEPS):
        weight = jnp.where(depth, columns[:, k : k + 1], 0.0)
        high, low = split(weight)
        wts[:count, k * nz : (k + 1) * nz] = high
        wts[count:, k * nz : (k + 1) * nz] = low

    def inject(start, end):
        length = end - start
        cells = lax.broadcasted_iota(jnp.int32, (length * ny, count), 0) + start * ny
        hit = jnp.where(cells == place, 1.0, 0.0).astype(BF16)
        hit = jnp.concatenate([hit, hit], axis=1)
        for k in range(0, STEPS, 2):
            added = dot(hit, wts[:, k * nz : (k + 2) * nz])
            for h in range(2):
                inj[k + h, start:end] = added[:, h * nz : (h + 1) * nz].reshape(length, ny, nz)

    def inject_until(done, end):
        while done < end:
            upto = min(done + CHUNK, end)
            inject(done, upto)
            done = upto
        return end

    injected = inject_until(halo, cuts[1] + 2 * halo - 1)

    loads[3].wait()
    at = lax.broadcasted_iota(jnp.int32, (ny, ny), 0)
    piece = at // ys
    inside = at - piece * ys
    side = inside // subs
    origin = (inside - side * subs) * (shots * part) + piece * part + side
    pick = jnp.where(origin == lax.broadcasted_iota(jnp.int32, (ny, ny), 1), 1.0, 0.0).astype(BF16)
    high, low = split(sy[...])
    high = dot(pick, high).astype(BF16)
    low = dot(pick, low).astype(BF16)
    syp[...] = jnp.concatenate([high, high, low], axis=1)

    pl.semaphore_wait(barrier, subs + shots - 2)

    def halo_copies(side):
        target = sub - 1 if side == 0 else sub + 1
        out = []
        for k, (src, dst, width) in enumerate(
            ((lam_cur.at[0], fa, halo), (lam_prev.at[0], fb, halo - 1), (courant, co, halo - 1))
        ):
            if side == 0:
                start, place = 0, halo + rows
            else:
                start, place = rows - width, halo - width
            out.append(pltpu.make_async_remote_copy(
                src_ref=src.at[pl.ds(start, width)],
                dst_ref=dst.at[pl.ds(place, width)],
                send_sem=halo_send.at[side, k],
                recv_sem=halo_recv.at[side, k],
                device_id=(shot, target),
                device_id_type=MESH,
            ))
        return out

    low_side = halo_copies(0)
    high_side = halo_copies(1)

    @pl.when(sub > 0)
    def _():
        for copy in low_side:
            copy.start()

    @pl.when(sub < subs - 1)
    def _():
        for copy in high_side:
            copy.start()

    @pl.when(sub == 0)
    def _():
        for ref in (fa, fb, co):
            ref[pl.ds(0, halo)] = jnp.zeros((halo, ny, nz), F32)

    @pl.when(sub == subs - 1)
    def _():
        for ref in (fa, fb, co):
            ref[pl.ds(halo + rows, halo)] = jnp.zeros((halo, ny, nz), F32)

    yi = lax.broadcasted_iota(jnp.int32, (ny, nz), 0)
    zi = lax.broadcasted_iota(jnp.int32, (ny, nz), 1)

    def fresh_row(k, e):
        src, dst = (fa, fb) if k % 2 == 0 else (fb, fa)
        mid = src[e]
        near = src[e - 1] + src[e + 1]
        near = near + jnp.where(yi == 0, 0.0, pltpu.roll(mid, 1, 0))
        near = near + jnp.where(yi == ny - 1, 0.0, pltpu.roll(mid, ny - 1, 0))
        near = near + jnp.where(zi == 0, 0.0, pltpu.roll(mid, 1, 1))
        near = near + jnp.where(zi == nz - 1, 0.0, pltpu.roll(mid, nz - 1, 1))
        speed = co[e]
        value = 2.0 * mid - dst[e] + speed * speed * (near - 6.0 * mid) + inj[k, e]
        dst[e] = value
        return value

    def image_row(k, x, value):
        term = value * ac[k, x].astype(F32)
        img[x] = term if k == 0 else img[x] + term

    sx0 = so[0, 0].astype(F32)
    dy = yi.astype(F32) - so[0, 1].astype(F32)
    dz = zi.astype(F32) - so[0, 2].astype(F32)
    flat = dy * dy + dz * dz

    def smooth_pair(x):
        planes = []
        for p in range(2):
            dx = (sub * rows + (x + p)).astype(F32) - sx0
            taper = 1.0 - jnp.exp(-(dx * dx + flat) / float(TAPER * TAPER))
            planes.append(img[x + p] * taper)
        out = dot(syp[...], stack3(jnp.concatenate(planes, axis=1), 0))
        for q in range(2):
            spot = pl.ds(slot(x + q) * subs, subs)
            for s in range(shots):
                for p in range(part):
                    at = s * ys + p * subs
                    stage[s, p, spot, :] = out[at : at + subs, q * nz : (q + 1) * nz]

    def slot(x):
        return x - halo if halo <= x < rows - halo else x + deep if x < halo else x

    def rs_copies(g):
        if g < groups:
            side, cut = slice(None), pl.ds(slot(cuts[g]) * subs, halo * subs)
        else:
            side, cut = g - groups, pl.ds(deep * subs, wide * subs)
        return [
            pltpu.make_async_remote_copy(
                src_ref=stage.at[peer, side, cut],
                dst_ref=gathered.at[d, side, cut],
                send_sem=rs_send.at[d, g],
                recv_sem=rs_recv.at[d, g],
                device_id=(peer, sub),
                device_id_type=MESH,
            )
            for d, peer in enumerate(peers)
        ]

    for copy in first_rows:
        copy.wait()
    sends = []
    for g in range(groups):
        if g == 1:
            for copy in other_rows:
                copy.wait()
        final_group = g == groups - 1
        injected = inject_until(injected, tall if final_group else cuts[g + 1] + 2 * halo - 1)
        if final_group:
            inject_until(0, halo)
        for k in range(STEPS):
            start = cuts[g] + halo - 1 - k if g else k + 1
            end = rows - 1 - k if final_group else cuts[g + 1] + halo - 1 - k
            for x in range(start, end):
                image_row(k, x, fresh_row(k, x + halo))

        for i in range(halo // 2):
            smooth_pair(cuts[g] + 2 * i)
        sends.append(rs_copies(g))
        for copy in sends[g]:
            copy.start()

    @pl.when(sub > 0)
    def _():
        for copy in high_side:
            copy.wait_recv()
        for copy in low_side:
            copy.wait_send()

    @pl.when(sub < subs - 1)
    def _():
        for copy in low_side:
            copy.wait_recv()
        for copy in high_side:
            copy.wait_send()

    for k in range(STEPS):
        for x in list(range(k + 1 - halo, k + 1)) + list(range(rows - 1 - k, rows - 1 - k + halo)):
            value = fresh_row(k, x + halo)
            if 0 <= x < rows:
                image_row(k, x, value)
    for x in list(range(0, halo, 2)) + list(range(rows - halo, rows, 2)):
        smooth_pair(x)
    for p in range(part):
        sends.append(rs_copies(groups + p))
        for copy in sends[groups + p]:
            copy.start()

    loads[4].wait()
    loads[5].wait()
    at = lax.broadcasted_iota(jnp.int32, (nx, 3 * nx), 1)
    block = at // (3 * subs * wide)
    place = at - block * (3 * subs * wide)
    term = place // (subs * wide)
    place = place - term * (subs * wide)
    where = place // wide
    place = place - where * wide
    edge = jnp.where(place < halo, place, place + deep)
    origin = where * rows + jnp.where(block < blocks - 1, halo + block * wide + place, edge)
    pick = jnp.where(origin == lax.broadcasted_iota(jnp.int32, (nx, 3 * nx), 0), 1.0, 0.0)
    high, low = split(sx[...])
    high = dot(high, jnp.where(term < 2, pick, 0.0).astype(BF16))
    low = dot(low, jnp.where(term < 2, 0.0, pick).astype(BF16))
    sxp[...] = (high + low).astype(BF16)
    high, low = split(jnp.transpose(sz[...]))
    szp[...] = jnp.concatenate([high, high, low], axis=0)

    def gather(b, p):
        for u in range(subs):
            cut = pl.ds(b * wide * subs + u, wide, stride=subs)
            total = stage[shot, p, cut, :]
            for d in range(shots - 1):
                total = total + gathered[d, p, cut, :]
            turned[b, p, u] = total

    def aa_copies(g):
        b, side = (g, slice(None)) if g < blocks - 1 else (blocks - 1, g - blocks + 1)
        spot = pl.ds(pl.multiple_of(sub * wide, 8), wide)
        out = []
        for d in range(1, subs):
            peer = lax.rem(sub + d, subs)
            out.append(pltpu.make_async_remote_copy(
                src_ref=turned.at[b, side, peer],
                dst_ref=lines.at[b, side, spot],
                send_sem=aa_send.at[d - 1, g],
                recv_sem=aa_recv.at[d - 1, g],
                device_id=(shot, peer),
                device_id_type=MESH,
            ))
        return out

    def keep(b, p):
        lines[b, p, pl.ds(pl.multiple_of(sub * wide, 8), wide), :] = turned[b, p, sub]

    def product(b, p):
        span = 3 * subs * wide
        return dot(sxp[:, b * span : (b + 1) * span], stack3(lines[b, p], 0))

    crossing = []
    for b in range(blocks - 1):
        for copies in sends[2 * b : 2 * b + 2]:
            for copy in copies:
                copy.wait_recv()
        for p in range(part):
            gather(b, p)
        crossing.append(aa_copies(b))
        for copy in crossing[b]:
            copy.start()
        for p in range(part):
            keep(b, p)
    for p in range(part):
        for copy in sends[groups + p]:
            copy.wait_recv()
        gather(blocks - 1, p)
        crossing.append(aa_copies(blocks - 1 + p))
        for copy in crossing[blocks - 1 + p]:
            copy.start()
        keep(blocks - 1, p)

    for b in range(blocks - 1):
        for copy in crossing[b]:
            copy.wait_recv()
        for p in range(part):
            value = product(b, p)
            held[p] = value if b == 0 else held[p] + value

    last = []
    for p in range(part):
        for copy in crossing[blocks - 1 + p]:
            copy.wait_recv()
        value = held[p] + product(blocks - 1, p)
        value = dot(stack3(value, 1), szp[...])
        ready[:, p] = value.reshape(shots, share, nz)
        for d, peer in enumerate(peers):
            copy = pltpu.make_async_remote_copy(
                src_ref=ready.at[peer, p],
                dst_ref=final.at[shot, p],
                send_sem=fin_send.at[d, p],
                recv_sem=fin_recv.at[d, p],
                device_id=(peer, sub),
                device_id_type=MESH,
            )
            copy.start()
            last.append(copy)
    final[shot] = ready[shot]
    for copies in sends + crossing:
        for copy in copies:
            copy.wait_send()
    for copy in last:
        copy.wait()


def place_kernel(pieces, newer, older, grad, prev_out, cur_out, outv, store_sem):
    rows = prev_out.shape[1]
    own = pl.ds((newer.shape[0] - rows) // 2, rows)
    stores = [
        pltpu.make_async_copy(older.at[own], prev_out.at[0], store_sem.at[0]),
        pltpu.make_async_copy(newer.at[own], cur_out.at[0], store_sem.at[1]),
    ]
    for copy in stores:
        copy.start()
    shots, part, share, _ = pieces.shape
    for s in range(shots):
        for p in range(part):
            outv[pl.ds(s * part + p, share, stride=shots * part), :] = pieces[s, p]
    put = pltpu.make_async_copy(outv, grad, store_sem.at[2])
    put.start()
    for copy in stores + [put]:
        copy.wait()


def fused(shots, subs, *args):
    courant, lam_prev, _, accel, traces, receivers, sources, smooth_x, smooth_y, smooth_z = args
    rows, ny, nz = courant.shape
    nx = smooth_x.shape[0]
    ys = ny // shots
    part = ys // subs
    share = nx // shots
    wide = 2 * STEPS
    tall = rows + wide
    blocks = rows // wide
    groups = (rows - wide) // STEPS
    field = lam_prev.shape
    receivers = jnp.transpose(receivers, (2, 0, 1))
    args = args[:5] + (receivers,) + args[6:]
    anywhere = pl.BlockSpec(memory_space=pltpu.HBM)
    dma = pltpu.SemaphoreType.DMA
    vmem = pl.BlockSpec(memory_space=pltpu.VMEM)
    grad, newer, older = pl.pallas_call(
        functools.partial(fused_kernel, shots, subs),
        out_shape=(
            pltpu.VMEM((shots, part, share, nz), F32),
            pltpu.VMEM((tall, ny, nz), F32),
            pltpu.VMEM((tall, ny, nz), F32),
        ),
        in_specs=[anywhere] * len(args),
        out_specs=(vmem,) * 3,
        scratch_shapes=[
            pltpu.VMEM((tall, ny, nz), F32),
            pltpu.VMEM(accel.shape[1:], accel.dtype),
            pltpu.VMEM(traces.shape[1:], F32),
            pltpu.VMEM(receivers.shape, jnp.int32),
            pltpu.SMEM(sources.shape, jnp.int32),
            pltpu.VMEM(smooth_x.shape, F32),
            pltpu.VMEM(smooth_y.shape, F32),
            pltpu.VMEM(smooth_z.shape, F32),
            pltpu.VMEM((STEPS, tall, ny, nz), F32),
            pltpu.VMEM((2 * receivers.shape[2], STEPS * nz), BF16),
            pltpu.VMEM((rows, ny, nz), F32),
            pltpu.VMEM((ny, 3 * ny), BF16),
            pltpu.VMEM((nx, 3 * nx), BF16),
            pltpu.VMEM((3 * nz, nz), BF16),
            pltpu.VMEM((shots, part, rows * subs, nz), F32),
            pltpu.VMEM((shots - 1, part, rows * subs, nz), F32),
            pltpu.VMEM((blocks, part, subs, wide, nz), F32),
            pltpu.VMEM((blocks, part, subs * wide, nz), F32),
            pltpu.VMEM((part, nx, nz), F32),
            pltpu.VMEM((shots, part, share, nz), F32),
            dma((14,)),
            dma((2, 3)),
            dma((2, 3)),
            dma((shots - 1, groups + part)),
            dma((shots - 1, groups + part)),
            dma((subs - 1, blocks - 1 + part)),
            dma((subs - 1, blocks - 1 + part)),
            dma((shots - 1, part)),
            dma((shots - 1, part)),
        ],
        compiler_params=pltpu.CompilerParams(
            collective_id=0, has_side_effects=True, vmem_limit_bytes=67043328 - 4 * (2 * tall * ny * nz + 2 * shots * part * share * nz)
        ),
    )(*args)
    grad, prev_out, cur_out = pl.pallas_call(
        place_kernel,
        out_shape=(
            jax.ShapeDtypeStruct((share * shots * part, nz), F32),
            jax.ShapeDtypeStruct(field, F32),
            jax.ShapeDtypeStruct(field, F32),
        ),
        in_specs=[vmem] * 3,
        out_specs=(anywhere,) * 3,
        scratch_shapes=[
            pltpu.VMEM((share * shots * part, nz), F32),
            dma((3,)),
        ],
        compiler_params=pltpu.CompilerParams(vmem_limit_bytes=8 * 2**20),
    )(grad, newer, older)
    return (grad.reshape(share, shots * part, nz), prev_out, cur_out)


def solution(mesh):
    in_specs = (
        P("sub", None, None),
        P("shot", "sub", None, None),
        P("shot", "sub", None, None),
        P("shot", None, "sub", None, None),
        P("shot", None, None),
        P("shot", None, None),
        P("shot", None),
        P(),
        P(),
        P(),
    )
    out_specs = (P("shot", "sub", None), P("shot", "sub", None, None), P("shot", "sub", None, None))
    shots, subs = mesh.shape["shot"], mesh.shape["sub"]

    def run(*args):
        courant, smooth_x, receivers = args[0], args[7], args[5]
        rows, ny, nz = courant.shape
        fits = (
            ny % (8 * shots) == 0
            and ny % (shots * subs) == 0
            and rows % 8 == 0
            and rows > 2 * STEPS
            and subs % 8 == 0
            and smooth_x.shape[0] % (8 * shots) == 0
            and nz % 128 == 0
            and shots > 1
            and subs > 1
        )
        return fused(shots, subs, *args) if fits else shards(*args)

    return jax.shard_map(run, mesh=mesh, in_specs=in_specs, out_specs=out_specs, check_vma=False)
```

```python
import functools

import jax
import jax.numpy as jnp
from jax import lax
from jax.experimental import pallas as pl
from jax.experimental.pallas import tpu as pltpu
from jax.sharding import PartitionSpec as P

STEPS = 4
TAPER = 8


def with_halo(value, sides, width):
    for axis, dim in sides:
        count, length = (lax.axis_size(axis), value.shape[dim])
        up = [(i, (i + 1) % count) for i in range(count - 1)]
        down = [(j, i) for i, j in up]
        last = lax.slice_in_dim(value, length - width, length, axis=dim)
        initial = lax.slice_in_dim(value, 0, width, axis=dim)
        before = lax.ppermute(last, axis, up)
        after = lax.ppermute(initial, axis, down)
        value = jnp.concatenate([before, value, after], axis=dim)
    return value


def plane_sum(block):
    side = jnp.pad(block, ((0, 0), (1, 1), (1, 1)))
    total = side[:, 2:, 1:-1] + side[:, :-2, 1:-1]
    return total + side[:, 1:-1, 2:] + side[:, 1:-1, :-2]


def inject(group_rec, weights, start, length, width_y, width_z):
    row_hit = (group_rec[None, :, 0] - start == jnp.arange(length)[:, None]).astype(jnp.float32)
    col_hit = (group_rec[None, :, 1] == jnp.arange(width_y)[:, None]).astype(jnp.float32)
    depth_hit = (group_rec[None, :, 2] == jnp.arange(width_z)[:, None]).astype(jnp.float32)
    plane = row_hit[:, None, :] * col_hit[None, :, :]
    depth_weight = depth_hit * weights[None, :]
    return jnp.einsum("abr,cr->abc", plane, depth_weight, precision=lax.Precision.HIGHEST)


def shards(
    courant, lam_prev, lam_cur, accel, traces, receivers, sources, smooth_x, smooth_y, smooth_z
):
    rows = courant.shape[0]
    width_y = courant.shape[1]
    width_z = courant.shape[2]
    first = lax.axis_index("sub") * rows
    coeff = courant * courant
    prev = lam_prev[0]
    cur = lam_cur[0]
    group_rec = receivers[0]
    image = jnp.zeros_like(cur)
    for step in range(STEPS):
        padded = with_halo(cur, (("sub", 0),), 1)
        beside = padded[2:] + padded[:-2] + plane_sum(cur)
        fresh = 2.0 * cur - prev + coeff * (beside - 6.0 * cur)
        fresh = fresh + inject(group_rec, traces[0, step], first, rows, width_y, width_z)
        image = image + fresh * accel[0, step].astype(jnp.float32)
        prev, cur = (cur, fresh)
    source = sources[0].astype(jnp.float32)
    xpos = (first + jnp.arange(rows)).astype(jnp.float32)[:, None, None]
    ypos = jnp.arange(width_y).astype(jnp.float32)[None, :, None]
    zpos = jnp.arange(width_z).astype(jnp.float32)[None, None, :]
    dist = (xpos - source[0]) ** 2 + (ypos - source[1]) ** 2 + (zpos - source[2]) ** 2
    image = image * (1.0 - jnp.exp(-dist / float(TAPER * TAPER)))
    high = lax.Precision.HIGHEST
    total = lax.psum(image, "shot")
    total = jnp.einsum("abc,kc->abk", total, smooth_z, precision=high)
    total = jnp.einsum("abk,jb->ajk", total, smooth_y, precision=high)
    lines = lax.all_to_all(total, "sub", split_axis=1, concat_axis=0, tiled=True)
    lines = jnp.einsum("ajk,ia->ijk", lines, smooth_x, precision=high)
    share = lines.shape[0] // lax.axis_size("shot")
    result = lax.dynamic_slice_in_dim(lines, lax.axis_index("shot") * share, share, 0)
    return (result, prev[None], cur[None])


MESH = pl.DeviceIdType.MESH
F32 = jnp.float32
BF16 = jnp.bfloat16


def split(value):
    high = value.astype(BF16)
    return high, (value - high.astype(F32)).astype(BF16)


def dot(a, b, dims=((1,), (0,))):
    return lax.dot_general(a, b, (dims, ((), ())), preferred_element_type=F32)


def dot3(a, b, dims=((1,), (0,))):
    (ah, al), (bh, bl) = a, b
    return dot(ah, bh, dims) + (dot(ah, bl, dims) + dot(al, bh, dims))


def stack3(value, axis):
    high, low = split(value)
    return jnp.concatenate([high, low, high], axis=axis)


def fused_kernel(
    shots, subs,
    courant, lam_prev, lam_cur, accel, traces, receivers, sources, smooth_x, smooth_y, smooth_z,
    final, fa, fb,
    co, ac, tr, rc, so, sx, sy, sz,
    inj, wts, img, syp, sxp, szp, stage, gathered, turned, lines, held, ready,
    local_sem, halo_send, halo_recv, rs_send, rs_recv, aa_send, aa_recv, fin_send, fin_recv,
):
    shot = lax.axis_index("shot")
    sub = lax.axis_index("sub")
    rows, ny, nz = courant.shape
    nx = smooth_x.shape[0]
    halo = STEPS
    ys = ny // shots
    part = ys // subs
    share = nx // shots
    cuts = [halo, halo + 2] + list(range(2 * halo, rows - halo + 1, halo))
    groups = len(cuts) - 1
    deep = rows - 2 * halo
    wide = 2 * halo
    tall = rows + wide
    blocks = rows // wide
    early = cuts[2] + halo

    def load(k, src, dst):
        copy = pltpu.make_async_copy(src, dst, local_sem.at[k])
        copy.start()
        return copy

    def pieces(k, start, length):
        here, there = pl.ds(start, length), pl.ds(halo + start, length)
        return [
            load(k, lam_cur.at[0, here], fa.at[there]),
            load(k + 1, lam_prev.at[0, here], fb.at[there]),
            load(k + 2, courant.at[here], co.at[there]),
            load(k + 3, accel.at[0, :, here], ac.at[:, here]),
        ]

    loads = [load(0, receivers, rc), load(1, traces.at[0], tr), load(2, sources, so)]
    first_rows = pieces(3, 0, early)
    loads.append(load(11, smooth_y, sy))
    other_rows = pieces(7, early, rows - early)
    loads += [load(12, smooth_x, sx), load(13, smooth_z, sz)]

    if shots == 4:
        peers = [3 - shot, shot + 1 - 2 * lax.rem(shot, 2), lax.rem(shot + 2, 4)]
    else:
        peers = [lax.rem(shot + d, shots) for d in range(1, shots)]

    barrier = pltpu.get_barrier_semaphore()
    for d in range(1, subs):
        pl.semaphore_signal(barrier, inc=1, device_id=(shot, lax.rem(sub + d, subs)), device_id_type=MESH)
    for peer in peers:
        pl.semaphore_signal(barrier, inc=1, device_id=(peer, sub), device_id_type=MESH)
    loads[0].wait()
    loads[1].wait()
    loads[2].wait()
    rec = rc[...]
    place = (rec[0] - (sub * rows - halo)) * ny + rec[1]
    count = rec.shape[2]
    level = jnp.transpose(jnp.broadcast_to(rec[2], (8, count)))
    depth = level[:, 0:1] == lax.broadcasted_iota(jnp.int32, (count, nz), 1)
    columns = jnp.transpose(tr[...])
    for k in range(STEPS):
        weight = jnp.where(depth, columns[:, k : k + 1], 0.0)
        high, low = split(weight)
        wts[:count, k * nz : (k + 1) * nz] = high
        wts[count:, k * nz : (k + 1) * nz] = low

    def inject(k, start, end):
        length = end - start
        if length <= 0:
            return
        cells = lax.broadcasted_iota(jnp.int32, (length * ny, count), 0) + start * ny
        hit = jnp.where(cells == place, 1.0, 0.0).astype(BF16)
        added = dot(jnp.concatenate([hit, hit], axis=1), wts[:, k * nz : (k + 2) * nz])
        for h in range(2):
            inj[k + h, start:end] = added[:, h * nz : (h + 1) * nz].reshape(length, ny, nz)

    def inject_for(g):
        for k in range(0, STEPS, 2):
            start = halo + k + 1 if g == 0 else cuts[g] + 2 * halo - 1 - k
            end = tall - 1 - k if g == groups - 1 else cuts[g + 1] + 2 * halo - 1 - k
            inject(k, start, end)
            if g == groups - 1:
                inject(k, k + 1, halo + k + 1)

    inject_for(0)

    pl.semaphore_wait(barrier, subs + shots - 2)

    def halo_copies(side):
        target = sub - 1 if side == 0 else sub + 1
        out = []
        for k, (src, dst, width) in enumerate(
            ((lam_cur.at[0], fa, halo), (lam_prev.at[0], fb, halo - 1), (courant, co, halo - 1))
        ):
            if side == 0:
                start, place = 0, halo + rows
            else:
                start, place = rows - width, halo - width
            out.append(pltpu.make_async_remote_copy(
                src_ref=src.at[pl.ds(start, width)],
                dst_ref=dst.at[pl.ds(place, width)],
                send_sem=halo_send.at[side, k],
                recv_sem=halo_recv.at[side, k],
                device_id=(shot, target),
                device_id_type=MESH,
            ))
        return out

    low_side = halo_copies(0)
    high_side = halo_copies(1)

    @pl.when(sub > 0)
    def _():
        for copy in low_side:
            copy.start()

    @pl.when(sub < subs - 1)
    def _():
        for copy in high_side:
            copy.start()

    @pl.when(sub == 0)
    def _():
        for ref in (fa, fb, co):
            ref[pl.ds(0, halo)] = jnp.zeros((halo, ny, nz), F32)

    @pl.when(sub == subs - 1)
    def _():
        for ref in (fa, fb, co):
            ref[pl.ds(halo + rows, halo)] = jnp.zeros((halo, ny, nz), F32)

    loads[3].wait()
    at = lax.broadcasted_iota(jnp.int32, (ny, ny), 0)
    piece = at // ys
    inside = at - piece * ys
    side = inside // subs
    origin = (inside - side * subs) * (shots * part) + piece * part + side
    pick = jnp.where(origin == lax.broadcasted_iota(jnp.int32, (ny, ny), 1), 1.0, 0.0).astype(BF16)
    high, low = split(sy[...])
    high = dot(pick, high).astype(BF16)
    low = dot(pick, low).astype(BF16)
    syp[...] = jnp.concatenate([high, high, low], axis=1)

    yi = lax.broadcasted_iota(jnp.int32, (ny, nz), 0)
    zi = lax.broadcasted_iota(jnp.int32, (ny, nz), 1)

    def fresh_row(k, e):
        src, dst = (fa, fb) if k % 2 == 0 else (fb, fa)
        mid = src[e]
        near = src[e - 1] + src[e + 1]
        near = near + jnp.where(yi == 0, 0.0, pltpu.roll(mid, 1, 0))
        near = near + jnp.where(yi == ny - 1, 0.0, pltpu.roll(mid, ny - 1, 0))
        near = near + jnp.where(zi == 0, 0.0, pltpu.roll(mid, 1, 1))
        near = near + jnp.where(zi == nz - 1, 0.0, pltpu.roll(mid, nz - 1, 1))
        speed = co[e]
        value = 2.0 * mid - dst[e] + speed * speed * (near - 6.0 * mid) + inj[k, e]
        dst[e] = value
        return value

    def image_row(k, x, value):
        term = value * ac[k, x].astype(F32)
        img[x] = term if k == 0 else img[x] + term

    sx0 = so[0, 0].astype(F32)
    dy = yi.astype(F32) - so[0, 1].astype(F32)
    dz = zi.astype(F32) - so[0, 2].astype(F32)
    flat = dy * dy + dz * dz

    def smooth_pair(x):
        planes = []
        for p in range(2):
            dx = (sub * rows + (x + p)).astype(F32) - sx0
            taper = 1.0 - jnp.exp(-(dx * dx + flat) / float(TAPER * TAPER))
            planes.append(img[x + p] * taper)
        out = dot(syp[...], stack3(jnp.concatenate(planes, axis=1), 0))
        for q in range(2):
            spot = pl.ds(slot(x + q) * subs, subs)
            for s in range(shots):
                for p in range(part):
                    at = s * ys + p * subs
                    stage[s, p, spot, :] = out[at : at + subs, q * nz : (q + 1) * nz]

    def slot(x):
        return x - halo if halo <= x < rows - halo else x + deep if x < halo else x

    def rs_copies(g):
        if g < groups:
            side, cut = slice(None), pl.ds(slot(cuts[g]) * subs, (cuts[g + 1] - cuts[g]) * subs)
        else:
            side, cut = g - groups, pl.ds(deep * subs, wide * subs)
        return [
            pltpu.make_async_remote_copy(
                src_ref=stage.at[peer, side, cut],
                dst_ref=gathered.at[d, side, cut],
                send_sem=rs_send.at[d, g],
                recv_sem=rs_recv.at[d, g],
                device_id=(peer, sub),
                device_id_type=MESH,
            )
            for d, peer in enumerate(peers)
        ]

    for copy in first_rows:
        copy.wait()
    sends = []
    for g in range(groups):
        if g == 2:
            for copy in other_rows:
                copy.wait()
        final_group = g == groups - 1
        if g > 0:
            inject_for(g)
        for k in range(STEPS):
            start = cuts[g] + halo - 1 - k if g else k + 1
            end = rows - 1 - k if final_group else cuts[g + 1] + halo - 1 - k
            for x in range(start, end):
                image_row(k, x, fresh_row(k, x + halo))

        for x in range(cuts[g], cuts[g + 1], 2):
            smooth_pair(x)
        sends.append(rs_copies(g))
        for copy in sends[g]:
            copy.start()

    @pl.when(sub > 0)
    def _():
        for copy in high_side:
            copy.wait_recv()
        for copy in low_side:
            copy.wait_send()

    @pl.when(sub < subs - 1)
    def _():
        for copy in low_side:
            copy.wait_recv()
        for copy in high_side:
            copy.wait_send()

    for k in range(STEPS):
        for x in list(range(k + 1 - halo, k + 1)) + list(range(rows - 1 - k, rows - 1 - k + halo)):
            value = fresh_row(k, x + halo)
            if 0 <= x < rows:
                image_row(k, x, value)
    for x in list(range(0, halo, 2)) + list(range(rows - halo, rows, 2)):
        smooth_pair(x)
    for p in range(part):
        sends.append(rs_copies(groups + p))
        for copy in sends[groups + p]:
            copy.start()

    loads[4].wait()
    loads[5].wait()
    at = lax.broadcasted_iota(jnp.int32, (nx, 3 * nx), 1)
    block = at // (3 * subs * wide)
    place = at - block * (3 * subs * wide)
    term = place // (subs * wide)
    place = place - term * (subs * wide)
    where = place // wide
    place = place - where * wide
    edge = jnp.where(place < halo, place, place + deep)
    origin = where * rows + jnp.where(block < blocks - 1, halo + block * wide + place, edge)
    pick = jnp.where(origin == lax.broadcasted_iota(jnp.int32, (nx, 3 * nx), 0), 1.0, 0.0)
    high, low = split(sx[...])
    high = dot(high, jnp.where(term < 2, pick, 0.0).astype(BF16))
    low = dot(low, jnp.where(term < 2, 0.0, pick).astype(BF16))
    sxp[...] = (high + low).astype(BF16)
    high, low = split(jnp.transpose(sz[...]))
    szp[...] = jnp.concatenate([high, high, low], axis=0)

    def gather(b, p):
        for u in range(subs):
            cut = pl.ds(b * wide * subs + u, wide, stride=subs)
            total = stage[shot, p, cut, :]
            for d in range(shots - 1):
                total = total + gathered[d, p, cut, :]
            turned[b, p, u] = total

    def aa_copies(g):
        b, side = (g, slice(None)) if g < blocks - 1 else (blocks - 1, g - blocks + 1)
        spot = pl.ds(pl.multiple_of(sub * wide, 8), wide)
        out = []
        for d in range(1, subs):
            peer = lax.rem(sub + d, subs)
            out.append(pltpu.make_async_remote_copy(
                src_ref=turned.at[b, side, peer],
                dst_ref=lines.at[b, side, spot],
                send_sem=aa_send.at[d - 1, g],
                recv_sem=aa_recv.at[d - 1, g],
                device_id=(shot, peer),
                device_id_type=MESH,
            ))
        return out

    def keep(b, p):
        lines[b, p, pl.ds(pl.multiple_of(sub * wide, 8), wide), :] = turned[b, p, sub]

    def product(b, p):
        span = 3 * subs * wide
        return dot(sxp[:, b * span : (b + 1) * span], stack3(lines[b, p], 0))

    crossing = []
    for b in range(blocks - 1):
        for copies in sends[2 * b + 1 if b else 0 : 2 * b + 3]:
            for copy in copies:
                copy.wait_recv()
        for p in range(part):
            gather(b, p)
        crossing.append(aa_copies(b))
        for copy in crossing[b]:
            copy.start()
        for p in range(part):
            keep(b, p)
    for p in range(part):
        for copy in sends[groups + p]:
            copy.wait_recv()
        gather(blocks - 1, p)
        crossing.append(aa_copies(blocks - 1 + p))
        for copy in crossing[blocks - 1 + p]:
            copy.start()
        keep(blocks - 1, p)

    for b in range(blocks - 1):
        for copy in crossing[b]:
            copy.wait_recv()
        for p in range(part):
            value = product(b, p)
            held[p] = value if b == 0 else held[p] + value

    last = []
    for p in range(part):
        for copy in crossing[blocks - 1 + p]:
            copy.wait_recv()
        value = held[p] + product(blocks - 1, p)
        value = dot(stack3(value, 1), szp[...])
        ready[:, p] = value.reshape(shots, share, nz)
        for d, peer in enumerate(peers):
            copy = pltpu.make_async_remote_copy(
                src_ref=ready.at[peer, p],
                dst_ref=final.at[shot, p],
                send_sem=fin_send.at[d, p],
                recv_sem=fin_recv.at[d, p],
                device_id=(peer, sub),
                device_id_type=MESH,
            )
            copy.start()
            last.append(copy)
    final[shot] = ready[shot]
    for copies in sends + crossing:
        for copy in copies:
            copy.wait_send()
    for copy in last:
        copy.wait()


def place_kernel(pieces, newer, older, grad, prev_out, cur_out, outv, store_sem):
    rows = prev_out.shape[1]
    own = pl.ds((newer.shape[0] - rows) // 2, rows)
    stores = [
        pltpu.make_async_copy(older.at[own], prev_out.at[0], store_sem.at[0]),
        pltpu.make_async_copy(newer.at[own], cur_out.at[0], store_sem.at[1]),
    ]
    for copy in stores:
        copy.start()
    shots, part, share, _ = pieces.shape
    for s in range(shots):
        for p in range(part):
            outv[pl.ds(s * part + p, share, stride=shots * part), :] = pieces[s, p]
    put = pltpu.make_async_copy(outv, grad, store_sem.at[2])
    put.start()
    for copy in stores + [put]:
        copy.wait()


def fused(shots, subs, *args):
    courant, lam_prev, _, accel, traces, receivers, sources, smooth_x, smooth_y, smooth_z = args
    rows, ny, nz = courant.shape
    nx = smooth_x.shape[0]
    ys = ny // shots
    part = ys // subs
    share = nx // shots
    wide = 2 * STEPS
    tall = rows + wide
    blocks = rows // wide
    groups = (rows - wide) // STEPS + 1
    field = lam_prev.shape
    receivers = jnp.transpose(receivers, (2, 0, 1))
    args = args[:5] + (receivers,) + args[6:]
    anywhere = pl.BlockSpec(memory_space=pltpu.HBM)
    dma = pltpu.SemaphoreType.DMA
    vmem = pl.BlockSpec(memory_space=pltpu.VMEM)
    grad, newer, older = pl.pallas_call(
        functools.partial(fused_kernel, shots, subs),
        out_shape=(
            pltpu.VMEM((shots, part, share, nz), F32),
            pltpu.VMEM((tall, ny, nz), F32),
            pltpu.VMEM((tall, ny, nz), F32),
        ),
        in_specs=[anywhere] * len(args),
        out_specs=(vmem,) * 3,
        scratch_shapes=[
            pltpu.VMEM((tall, ny, nz), F32),
            pltpu.VMEM(accel.shape[1:], accel.dtype),
            pltpu.VMEM(traces.shape[1:], F32),
            pltpu.VMEM(receivers.shape, jnp.int32),
            pltpu.SMEM(sources.shape, jnp.int32),
            pltpu.VMEM(smooth_x.shape, F32),
            pltpu.VMEM(smooth_y.shape, F32),
            pltpu.VMEM(smooth_z.shape, F32),
            pltpu.VMEM((STEPS, tall, ny, nz), F32),
            pltpu.VMEM((2 * receivers.shape[2], STEPS * nz), BF16),
            pltpu.VMEM((rows, ny, nz), F32),
            pltpu.VMEM((ny, 3 * ny), BF16),
            pltpu.VMEM((nx, 3 * nx), BF16),
            pltpu.VMEM((3 * nz, nz), BF16),
            pltpu.VMEM((shots, part, rows * subs, nz), F32),
            pltpu.VMEM((shots - 1, part, rows * subs, nz), F32),
            pltpu.VMEM((blocks, part, subs, wide, nz), F32),
            pltpu.VMEM((blocks, part, subs * wide, nz), F32),
            pltpu.VMEM((part, nx, nz), F32),
            pltpu.VMEM((shots, part, share, nz), F32),
            dma((14,)),
            dma((2, 3)),
            dma((2, 3)),
            dma((shots - 1, groups + part)),
            dma((shots - 1, groups + part)),
            dma((subs - 1, blocks - 1 + part)),
            dma((subs - 1, blocks - 1 + part)),
            dma((shots - 1, part)),
            dma((shots - 1, part)),
        ],
        compiler_params=pltpu.CompilerParams(
            collective_id=0, has_side_effects=True, vmem_limit_bytes=67043328 - 4 * (2 * tall * ny * nz + 2 * shots * part * share * nz)
        ),
    )(*args)
    grad, prev_out, cur_out = pl.pallas_call(
        place_kernel,
        out_shape=(
            jax.ShapeDtypeStruct((share * shots * part, nz), F32),
            jax.ShapeDtypeStruct(field, F32),
            jax.ShapeDtypeStruct(field, F32),
        ),
        in_specs=[vmem] * 3,
        out_specs=(anywhere,) * 3,
        scratch_shapes=[
            pltpu.VMEM((share * shots * part, nz), F32),
            dma((3,)),
        ],
        compiler_params=pltpu.CompilerParams(vmem_limit_bytes=8 * 2**20),
    )(grad, newer, older)
    return (grad.reshape(share, shots * part, nz), prev_out, cur_out)


def solution(mesh):
    in_specs = (
        P("sub", None, None),
        P("shot", "sub", None, None),
        P("shot", "sub", None, None),
        P("shot", None, "sub", None, None),
        P("shot", None, None),
        P("shot", None, None),
        P("shot", None),
        P(),
        P(),
        P(),
    )
    out_specs = (P("shot", "sub", None), P("shot", "sub", None, None), P("shot", "sub", None, None))
    shots, subs = mesh.shape["shot"], mesh.shape["sub"]

    def run(*args):
        courant, smooth_x, receivers = args[0], args[7], args[5]
        rows, ny, nz = courant.shape
        fits = (
            ny % (8 * shots) == 0
            and ny % (shots * subs) == 0
            and rows % 8 == 0
            and rows > 2 * STEPS
            and subs % 8 == 0
            and smooth_x.shape[0] % (8 * shots) == 0
            and nz % 128 == 0
            and shots > 1
            and subs > 1
        )
        return fused(shots, subs, *args) if fits else shards(*args)

    return jax.shard_map(run, mesh=mesh, in_specs=in_specs, out_specs=out_specs, check_vma=False)
```

```python
import functools

import jax
import jax.numpy as jnp
from jax import lax
from jax.experimental import pallas as pl
from jax.experimental.pallas import tpu as pltpu
from jax.sharding import PartitionSpec as P

STEPS = 4
TAPER = 8


def with_halo(value, sides, width):
    for axis, dim in sides:
        count, length = (lax.axis_size(axis), value.shape[dim])
        up = [(i, (i + 1) % count) for i in range(count - 1)]
        down = [(j, i) for i, j in up]
        last = lax.slice_in_dim(value, length - width, length, axis=dim)
        initial = lax.slice_in_dim(value, 0, width, axis=dim)
        before = lax.ppermute(last, axis, up)
        after = lax.ppermute(initial, axis, down)
        value = jnp.concatenate([before, value, after], axis=dim)
    return value


def plane_sum(block):
    side = jnp.pad(block, ((0, 0), (1, 1), (1, 1)))
    total = side[:, 2:, 1:-1] + side[:, :-2, 1:-1]
    return total + side[:, 1:-1, 2:] + side[:, 1:-1, :-2]


def inject(group_rec, weights, start, length, width_y, width_z):
    row_hit = (group_rec[None, :, 0] - start == jnp.arange(length)[:, None]).astype(jnp.float32)
    col_hit = (group_rec[None, :, 1] == jnp.arange(width_y)[:, None]).astype(jnp.float32)
    depth_hit = (group_rec[None, :, 2] == jnp.arange(width_z)[:, None]).astype(jnp.float32)
    plane = row_hit[:, None, :] * col_hit[None, :, :]
    depth_weight = depth_hit * weights[None, :]
    return jnp.einsum("abr,cr->abc", plane, depth_weight, precision=lax.Precision.HIGHEST)


def shards(
    courant, lam_prev, lam_cur, accel, traces, receivers, sources, smooth_x, smooth_y, smooth_z
):
    rows = courant.shape[0]
    width_y = courant.shape[1]
    width_z = courant.shape[2]
    first = lax.axis_index("sub") * rows
    coeff = courant * courant
    prev = lam_prev[0]
    cur = lam_cur[0]
    group_rec = receivers[0]
    image = jnp.zeros_like(cur)
    for step in range(STEPS):
        padded = with_halo(cur, (("sub", 0),), 1)
        beside = padded[2:] + padded[:-2] + plane_sum(cur)
        fresh = 2.0 * cur - prev + coeff * (beside - 6.0 * cur)
        fresh = fresh + inject(group_rec, traces[0, step], first, rows, width_y, width_z)
        image = image + fresh * accel[0, step].astype(jnp.float32)
        prev, cur = (cur, fresh)
    source = sources[0].astype(jnp.float32)
    xpos = (first + jnp.arange(rows)).astype(jnp.float32)[:, None, None]
    ypos = jnp.arange(width_y).astype(jnp.float32)[None, :, None]
    zpos = jnp.arange(width_z).astype(jnp.float32)[None, None, :]
    dist = (xpos - source[0]) ** 2 + (ypos - source[1]) ** 2 + (zpos - source[2]) ** 2
    image = image * (1.0 - jnp.exp(-dist / float(TAPER * TAPER)))
    high = lax.Precision.HIGHEST
    total = lax.psum(image, "shot")
    total = jnp.einsum("abc,kc->abk", total, smooth_z, precision=high)
    total = jnp.einsum("abk,jb->ajk", total, smooth_y, precision=high)
    lines = lax.all_to_all(total, "sub", split_axis=1, concat_axis=0, tiled=True)
    lines = jnp.einsum("ajk,ia->ijk", lines, smooth_x, precision=high)
    share = lines.shape[0] // lax.axis_size("shot")
    result = lax.dynamic_slice_in_dim(lines, lax.axis_index("shot") * share, share, 0)
    return (result, prev[None], cur[None])


MESH = pl.DeviceIdType.MESH
F32 = jnp.float32
BF16 = jnp.bfloat16


def split(value):
    high = value.astype(BF16)
    return high, (value - high.astype(F32)).astype(BF16)


def dot(a, b, dims=((1,), (0,))):
    return lax.dot_general(a, b, (dims, ((), ())), preferred_element_type=F32)


def dot3(a, b, dims=((1,), (0,))):
    (ah, al), (bh, bl) = a, b
    return dot(ah, bh, dims) + (dot(ah, bl, dims) + dot(al, bh, dims))


def stack3(value, axis):
    high, low = split(value)
    return jnp.concatenate([high, low, high], axis=axis)


def fused_kernel(
    shots, subs,
    courant, lam_prev, lam_cur, accel, traces, receivers, sources, smooth_x, smooth_y, smooth_z,
    final, fa, fb,
    co, ac, tr, rc, so, sx, sy, sz,
    inj, wts, img, syp, sxp, szp, stage, gathered, turned, lines, held, ready,
    local_sem, halo_send, halo_recv, rs_send, rs_recv, aa_send, aa_recv, fin_send, fin_recv,
):
    shot = lax.axis_index("shot")
    sub = lax.axis_index("sub")
    rows, ny, nz = courant.shape
    nx = smooth_x.shape[0]
    halo = STEPS
    ys = ny // shots
    part = ys // subs
    share = nx // shots
    cuts = [halo, halo + 2] + list(range(2 * halo, rows - halo + 1, halo))
    groups = len(cuts) - 1
    deep = rows - 2 * halo
    wide = 2 * halo
    tall = rows + wide
    blocks = rows // wide
    early = cuts[1] + halo

    def load(k, src, dst):
        copy = pltpu.make_async_copy(src, dst, local_sem.at[k])
        copy.start()
        return copy

    def pieces(k, start, length):
        here, there = pl.ds(start, length), pl.ds(halo + start, length)
        return [
            load(k, lam_cur.at[0, here], fa.at[there]),
            load(k + 1, lam_prev.at[0, here], fb.at[there]),
            load(k + 2, courant.at[here], co.at[there]),
            load(k + 3, accel.at[0, :, here], ac.at[:, here]),
        ]

    loads = [load(0, receivers, rc), load(1, traces.at[0], tr), load(2, sources, so)]
    first_rows = pieces(3, 0, early)
    loads.append(load(11, smooth_y, sy))
    other_rows = pieces(7, early, rows - early)
    loads += [load(12, smooth_x, sx), load(13, smooth_z, sz)]

    if shots == 4:
        peers = [3 - shot, shot + 1 - 2 * lax.rem(shot, 2), lax.rem(shot + 2, 4)]
    else:
        peers = [lax.rem(shot + d, shots) for d in range(1, shots)]

    barrier = pltpu.get_barrier_semaphore()
    for d in range(1, subs):
        pl.semaphore_signal(barrier, inc=1, device_id=(shot, lax.rem(sub + d, subs)), device_id_type=MESH)
    for peer in peers:
        pl.semaphore_signal(barrier, inc=1, device_id=(peer, sub), device_id_type=MESH)
    loads[0].wait()
    loads[1].wait()
    loads[2].wait()
    rec = rc[...]
    place = (rec[0] - (sub * rows - halo)) * ny + rec[1]
    count = rec.shape[2]
    level = jnp.transpose(jnp.broadcast_to(rec[2], (8, count)))
    depth = level[:, 0:1] == lax.broadcasted_iota(jnp.int32, (count, nz), 1)
    columns = jnp.transpose(tr[...])
    for k in range(STEPS):
        weight = jnp.where(depth, columns[:, k : k + 1], 0.0)
        high, low = split(weight)
        wts[:count, k * nz : (k + 1) * nz] = high
        wts[count:, k * nz : (k + 1) * nz] = low

    def inject(k, start, end):
        length = end - start
        if length <= 0:
            return
        cells = lax.broadcasted_iota(jnp.int32, (length * ny, count), 0) + start * ny
        hit = jnp.where(cells == place, 1.0, 0.0).astype(BF16)
        added = dot(jnp.concatenate([hit, hit], axis=1), wts[:, k * nz : (k + 2) * nz])
        for h in range(2):
            inj[k + h, start:end] = added[:, h * nz : (h + 1) * nz].reshape(length, ny, nz)

    def inject_for(g):
        for k in range(0, STEPS, 2):
            start = halo + k + 1 if g == 0 else cuts[g] + 2 * halo - 1 - k
            end = tall - 1 - k if g == groups - 1 else cuts[g + 1] + 2 * halo - 1 - k
            inject(k, start, end)
            if g == groups - 1:
                inject(k, k + 1, halo + k + 1)

    inject_for(0)

    pl.semaphore_wait(barrier, subs + shots - 2)

    def halo_copies(side):
        target = sub - 1 if side == 0 else sub + 1
        out = []
        for k, (src, dst, width) in enumerate(
            ((lam_cur.at[0], fa, halo), (lam_prev.at[0], fb, halo - 1), (courant, co, halo - 1))
        ):
            if side == 0:
                start, place = 0, halo + rows
            else:
                start, place = rows - width, halo - width
            out.append(pltpu.make_async_remote_copy(
                src_ref=src.at[pl.ds(start, width)],
                dst_ref=dst.at[pl.ds(place, width)],
                send_sem=halo_send.at[side, k],
                recv_sem=halo_recv.at[side, k],
                device_id=(shot, target),
                device_id_type=MESH,
            ))
        return out

    low_side = halo_copies(0)
    high_side = halo_copies(1)

    @pl.when(sub > 0)
    def _():
        for copy in low_side:
            copy.start()

    @pl.when(sub < subs - 1)
    def _():
        for copy in high_side:
            copy.start()

    @pl.when(sub == 0)
    def _():
        for ref in (fa, fb, co):
            ref[pl.ds(0, halo)] = jnp.zeros((halo, ny, nz), F32)

    @pl.when(sub == subs - 1)
    def _():
        for ref in (fa, fb, co):
            ref[pl.ds(halo + rows, halo)] = jnp.zeros((halo, ny, nz), F32)

    loads[3].wait()
    at = lax.broadcasted_iota(jnp.int32, (ny, ny), 0)
    piece = at // ys
    inside = at - piece * ys
    side = inside // subs
    origin = (inside - side * subs) * (shots * part) + piece * part + side
    pick = jnp.where(origin == lax.broadcasted_iota(jnp.int32, (ny, ny), 1), 1.0, 0.0).astype(BF16)
    high, low = split(sy[...])
    high = dot(pick, high).astype(BF16)
    low = dot(pick, low).astype(BF16)
    syp[...] = jnp.concatenate([high, high, low], axis=1)

    yi = lax.broadcasted_iota(jnp.int32, (ny, nz), 0)
    zi = lax.broadcasted_iota(jnp.int32, (ny, nz), 1)

    def fresh_row(k, e):
        src, dst = (fa, fb) if k % 2 == 0 else (fb, fa)
        mid = src[e]
        near = src[e - 1] + src[e + 1]
        near = near + jnp.where(yi == 0, 0.0, pltpu.roll(mid, 1, 0))
        near = near + jnp.where(yi == ny - 1, 0.0, pltpu.roll(mid, ny - 1, 0))
        near = near + jnp.where(zi == 0, 0.0, pltpu.roll(mid, 1, 1))
        near = near + jnp.where(zi == nz - 1, 0.0, pltpu.roll(mid, nz - 1, 1))
        speed = co[e]
        value = 2.0 * mid - dst[e] + speed * speed * (near - 6.0 * mid) + inj[k, e]
        dst[e] = value
        return value

    def image_row(k, x, value):
        term = value * ac[k, x].astype(F32)
        img[x] = term if k == 0 else img[x] + term

    sx0 = so[0, 0].astype(F32)
    dy = yi.astype(F32) - so[0, 1].astype(F32)
    dz = zi.astype(F32) - so[0, 2].astype(F32)
    flat = dy * dy + dz * dz

    def smooth_pair(x):
        planes = []
        for p in range(2):
            dx = (sub * rows + (x + p)).astype(F32) - sx0
            taper = 1.0 - jnp.exp(-(dx * dx + flat) / float(TAPER * TAPER))
            planes.append(img[x + p] * taper)
        out = dot(syp[...], stack3(jnp.concatenate(planes, axis=1), 0))
        for q in range(2):
            spot = pl.ds(slot(x + q) * subs, subs)
            for s in range(shots):
                for p in range(part):
                    at = s * ys + p * subs
                    stage[s, p, spot, :] = out[at : at + subs, q * nz : (q + 1) * nz]

    def slot(x):
        return x - halo if halo <= x < rows - halo else x + deep if x < halo else x

    def rs_copies(g):
        if g < groups:
            side, cut = slice(None), pl.ds(slot(cuts[g]) * subs, (cuts[g + 1] - cuts[g]) * subs)
        else:
            side, cut = g - groups, pl.ds(deep * subs, wide * subs)
        return [
            pltpu.make_async_remote_copy(
                src_ref=stage.at[peer, side, cut],
                dst_ref=gathered.at[d, side, cut],
                send_sem=rs_send.at[d, g],
                recv_sem=rs_recv.at[d, g],
                device_id=(peer, sub),
                device_id_type=MESH,
            )
            for d, peer in enumerate(peers)
        ]

    for copy in first_rows:
        copy.wait()
    sends = []
    for g in range(groups):
        if g == 1:
            for copy in other_rows:
                copy.wait()
        final_group = g == groups - 1
        if g > 0:
            inject_for(g)
        for k in range(STEPS):
            start = cuts[g] + halo - 1 - k if g else k + 1
            end = rows - 1 - k if final_group else cuts[g + 1] + halo - 1 - k
            for x in range(start, end):
                image_row(k, x, fresh_row(k, x + halo))

        for x in range(cuts[g], cuts[g + 1], 2):
            smooth_pair(x)
        sends.append(rs_copies(g))
        for copy in sends[g]:
            copy.start()

    @pl.when(sub > 0)
    def _():
        for copy in high_side:
            copy.wait_recv()
        for copy in low_side:
            copy.wait_send()

    @pl.when(sub < subs - 1)
    def _():
        for copy in low_side:
            copy.wait_recv()
        for copy in high_side:
            copy.wait_send()

    for k in range(STEPS):
        for x in list(range(k + 1 - halo, k + 1)) + list(range(rows - 1 - k, rows - 1 - k + halo)):
            value = fresh_row(k, x + halo)
            if 0 <= x < rows:
                image_row(k, x, value)
    for x in list(range(0, halo, 2)) + list(range(rows - halo, rows, 2)):
        smooth_pair(x)
    for p in range(part):
        sends.append(rs_copies(groups + p))
        for copy in sends[groups + p]:
            copy.start()

    loads[4].wait()
    loads[5].wait()
    at = lax.broadcasted_iota(jnp.int32, (nx, 3 * nx), 1)
    block = at // (3 * subs * wide)
    place = at - block * (3 * subs * wide)
    term = place // (subs * wide)
    place = place - term * (subs * wide)
    where = place // wide
    place = place - where * wide
    edge = jnp.where(place < halo, place, place + deep)
    origin = where * rows + jnp.where(block < blocks - 1, halo + block * wide + place, edge)
    pick = jnp.where(origin == lax.broadcasted_iota(jnp.int32, (nx, 3 * nx), 0), 1.0, 0.0)
    high, low = split(sx[...])
    high = dot(high, jnp.where(term < 2, pick, 0.0).astype(BF16))
    low = dot(low, jnp.where(term < 2, 0.0, pick).astype(BF16))
    sxp[...] = (high + low).astype(BF16)
    high, low = split(jnp.transpose(sz[...]))
    szp[...] = jnp.concatenate([high, high, low], axis=0)

    def gather(b, p):
        for u in range(subs):
            cut = pl.ds(b * wide * subs + u, wide, stride=subs)
            total = stage[shot, p, cut, :]
            for d in range(shots - 1):
                total = total + gathered[d, p, cut, :]
            turned[b, p, u] = total

    def aa_copies(g):
        b, side = (g, slice(None)) if g < blocks - 1 else (blocks - 1, g - blocks + 1)
        spot = pl.ds(pl.multiple_of(sub * wide, 8), wide)
        out = []
        for d in range(1, subs):
            peer = lax.rem(sub + d, subs)
            out.append(pltpu.make_async_remote_copy(
                src_ref=turned.at[b, side, peer],
                dst_ref=lines.at[b, side, spot],
                send_sem=aa_send.at[d - 1, g],
                recv_sem=aa_recv.at[d - 1, g],
                device_id=(shot, peer),
                device_id_type=MESH,
            ))
        return out

    def keep(b, p):
        lines[b, p, pl.ds(pl.multiple_of(sub * wide, 8), wide), :] = turned[b, p, sub]

    def product(b, p):
        span = 3 * subs * wide
        return dot(sxp[:, b * span : (b + 1) * span], stack3(lines[b, p], 0))

    crossing = []
    for b in range(blocks - 1):
        for copies in sends[2 * b + 1 if b else 0 : 2 * b + 3]:
            for copy in copies:
                copy.wait_recv()
        for p in range(part):
            gather(b, p)
        crossing.append(aa_copies(b))
        for copy in crossing[b]:
            copy.start()
        for p in range(part):
            keep(b, p)
    for p in range(part):
        for copy in sends[groups + p]:
            copy.wait_recv()
        gather(blocks - 1, p)
        crossing.append(aa_copies(blocks - 1 + p))
        for copy in crossing[blocks - 1 + p]:
            copy.start()
        keep(blocks - 1, p)

    for b in range(blocks - 1):
        for copy in crossing[b]:
            copy.wait_recv()
        for p in range(part):
            value = product(b, p)
            held[p] = value if b == 0 else held[p] + value

    last = []
    for p in range(part):
        for copy in crossing[blocks - 1 + p]:
            copy.wait_recv()
        value = held[p] + product(blocks - 1, p)
        value = dot(stack3(value, 1), szp[...])
        ready[:, p] = value.reshape(shots, share, nz)
        for d, peer in enumerate(peers):
            copy = pltpu.make_async_remote_copy(
                src_ref=ready.at[peer, p],
                dst_ref=final.at[shot, p],
                send_sem=fin_send.at[d, p],
                recv_sem=fin_recv.at[d, p],
                device_id=(peer, sub),
                device_id_type=MESH,
            )
            copy.start()
            last.append(copy)
    final[shot] = ready[shot]
    for copies in sends + crossing:
        for copy in copies:
            copy.wait_send()
    for copy in last:
        copy.wait()


def place_kernel(pieces, newer, older, grad, prev_out, cur_out, outv, store_sem):
    rows = prev_out.shape[1]
    own = pl.ds((newer.shape[0] - rows) // 2, rows)
    stores = [
        pltpu.make_async_copy(older.at[own], prev_out.at[0], store_sem.at[0]),
        pltpu.make_async_copy(newer.at[own], cur_out.at[0], store_sem.at[1]),
    ]
    for copy in stores:
        copy.start()
    shots, part, share, _ = pieces.shape
    for s in range(shots):
        for p in range(part):
            outv[pl.ds(s * part + p, share, stride=shots * part), :] = pieces[s, p]
    put = pltpu.make_async_copy(outv, grad, store_sem.at[2])
    put.start()
    for copy in stores + [put]:
        copy.wait()


def fused(shots, subs, *args):
    courant, lam_prev, _, accel, traces, receivers, sources, smooth_x, smooth_y, smooth_z = args
    rows, ny, nz = courant.shape
    nx = smooth_x.shape[0]
    ys = ny // shots
    part = ys // subs
    share = nx // shots
    wide = 2 * STEPS
    tall = rows + wide
    blocks = rows // wide
    groups = (rows - wide) // STEPS + 1
    field = lam_prev.shape
    receivers = jnp.transpose(receivers, (2, 0, 1))
    args = args[:5] + (receivers,) + args[6:]
    anywhere = pl.BlockSpec(memory_space=pltpu.HBM)
    dma = pltpu.SemaphoreType.DMA
    vmem = pl.BlockSpec(memory_space=pltpu.VMEM)
    grad, newer, older = pl.pallas_call(
        functools.partial(fused_kernel, shots, subs),
        out_shape=(
            pltpu.VMEM((shots, part, share, nz), F32),
            pltpu.VMEM((tall, ny, nz), F32),
            pltpu.VMEM((tall, ny, nz), F32),
        ),
        in_specs=[anywhere] * len(args),
        out_specs=(vmem,) * 3,
        scratch_shapes=[
            pltpu.VMEM((tall, ny, nz), F32),
            pltpu.VMEM(accel.shape[1:], accel.dtype),
            pltpu.VMEM(traces.shape[1:], F32),
            pltpu.VMEM(receivers.shape, jnp.int32),
            pltpu.SMEM(sources.shape, jnp.int32),
            pltpu.VMEM(smooth_x.shape, F32),
            pltpu.VMEM(smooth_y.shape, F32),
            pltpu.VMEM(smooth_z.shape, F32),
            pltpu.VMEM((STEPS, tall, ny, nz), F32),
            pltpu.VMEM((2 * receivers.shape[2], STEPS * nz), BF16),
            pltpu.VMEM((rows, ny, nz), F32),
            pltpu.VMEM((ny, 3 * ny), BF16),
            pltpu.VMEM((nx, 3 * nx), BF16),
            pltpu.VMEM((3 * nz, nz), BF16),
            pltpu.VMEM((shots, part, rows * subs, nz), F32),
            pltpu.VMEM((shots - 1, part, rows * subs, nz), F32),
            pltpu.VMEM((blocks, part, subs, wide, nz), F32),
            pltpu.VMEM((blocks, part, subs * wide, nz), F32),
            pltpu.VMEM((part, nx, nz), F32),
            pltpu.VMEM((shots, part, share, nz), F32),
            dma((14,)),
            dma((2, 3)),
            dma((2, 3)),
            dma((shots - 1, groups + part)),
            dma((shots - 1, groups + part)),
            dma((subs - 1, blocks - 1 + part)),
            dma((subs - 1, blocks - 1 + part)),
            dma((shots - 1, part)),
            dma((shots - 1, part)),
        ],
        compiler_params=pltpu.CompilerParams(
            collective_id=0, has_side_effects=True, vmem_limit_bytes=67043328 - 4 * (2 * tall * ny * nz + 2 * shots * part * share * nz)
        ),
    )(*args)
    grad, prev_out, cur_out = pl.pallas_call(
        place_kernel,
        out_shape=(
            jax.ShapeDtypeStruct((share * shots * part, nz), F32),
            jax.ShapeDtypeStruct(field, F32),
            jax.ShapeDtypeStruct(field, F32),
        ),
        in_specs=[vmem] * 3,
        out_specs=(anywhere,) * 3,
        scratch_shapes=[
            pltpu.VMEM((share * shots * part, nz), F32),
            dma((3,)),
        ],
        compiler_params=pltpu.CompilerParams(vmem_limit_bytes=8 * 2**20),
    )(grad, newer, older)
    return (grad.reshape(share, shots * part, nz), prev_out, cur_out)


def solution(mesh):
    in_specs = (
        P("sub", None, None),
        P("shot", "sub", None, None),
        P("shot", "sub", None, None),
        P("shot", None, "sub", None, None),
        P("shot", None, None),
        P("shot", None, None),
        P("shot", None),
        P(),
        P(),
        P(),
    )
    out_specs = (P("shot", "sub", None), P("shot", "sub", None, None), P("shot", "sub", None, None))
    shots, subs = mesh.shape["shot"], mesh.shape["sub"]

    def run(*args):
        courant, smooth_x, receivers = args[0], args[7], args[5]
        rows, ny, nz = courant.shape
        fits = (
            ny % (8 * shots) == 0
            and ny % (shots * subs) == 0
            and rows % 8 == 0
            and rows > 2 * STEPS
            and subs % 8 == 0
            and smooth_x.shape[0] % (8 * shots) == 0
            and nz % 128 == 0
            and shots > 1
            and subs > 1
        )
        return fused(shots, subs, *args) if fits else shards(*args)

    return jax.shard_map(run, mesh=mesh, in_specs=in_specs, out_specs=out_specs, check_vma=False)
```
